128 devices in a mesh: store: 8 (over z, core), mp: 16 (over y, x).
Axes of the slice: x: 4, y: 4, z: 4, core: 2. Of those that a mesh axis runs over, the one named last changes fastest.
Arguments:
- tokens: bfloat16 [2048, 6144], P('store', 'mp'), may hold values from -6 to 6
- gain: float32 [6144], replicated, may hold values from 0.1 to 1.9
- base_projection_weight: bfloat16 [6144, 6144], P(None, 'mp'), may hold values from -0.078125 to 0.078125
- adapter_down_weight: bfloat16 [64, 64, 6144], P('store', None, 'mp'), may hold values from -0.078125 to 0.078125
- adapter_up_weight: bfloat16 [64, 64, 6144], P('store', None, 'mp'), may hold values from -0.75 to 0.75
- plan: int32 [8, 4], replicated, may hold values from 0 to 63, as said below
- target: int32 [2048, 1], P('store'), may hold values from 0 to 7; in each aligned block of 256 rows (0 to 255, 256 to 511, ...) at most 64 rows name the same one
- slot: int32 [2048], P('store'), may hold values from 0 to 11
Outputs:
- hidden_out: bfloat16 [2048, 6144], P('store', 'mp')
The draws below stay inside these ranges and needn't reach their ends.
Inputs may be any that keep to these rules, and one draw needn't show every extreme that they name: plan[g, r] is an adapter owned by a store group other than g; adapter a is owned by group a // 8. `target`: among the 256 rows of one store group at most 64 name the same group, a bound that some block reaches.
All inputs are finite; a program needn't handle non-finite values.
Results may differ from the reference program's by a relative error of at most 0.0063.
Values may be sent and summed in bfloat16 or wider, within the bound.
A program may use at most 64 MiB of HBM per device.

```python
import math
import jax
import jax.numpy as jnp
import numpy as np
from jax import lax

MODEL_WIDTH = 6144
ADAPTER_RANK = 64
STEPS = 4
REPL = 4
ADP_GRP = 8
TOK_GRP = 256
CAP = 64
SLOTS = 12
ADAPTER_TOTAL = 64
TOKENS = 2048
N_STORE = 8


def draw_plan(key, part):
    groups = ADAPTER_TOTAL // ADP_GRP
    first_key = jax.random.fold_in(key, 11)
    second_key = jax.random.fold_in(key, 23)
    offset = jax.random.randint(first_key, (groups, REPL), 0, groups - 1)
    local = jax.random.randint(second_key, (groups, REPL), 0, ADP_GRP)
    owner = (jnp.arange(groups, dtype=jnp.int32)[:, None] + 1 + offset) % groups
    return (owner * ADP_GRP + local).astype(jnp.int32)


def plant(array, rng, least, high):
    extent = array.shape
    place = [jax.random.randint(jax.random.fold_in(rng, axis), (), 0, extent[axis]) for axis in range(len(extent))]
    array = array.at[tuple(place)].set(least)
    longest = extent.index(max(extent))
    place[longest] = (place[longest] + 1) % extent[longest]
    return array.at[tuple(place)].set(high)


def block_levels(rng, dims, pieces, least, top_value):
    factor_of = 1.0
    for dim, blocks in pieces:
        steps = jax.random.uniform(jax.random.fold_in(jax.random.fold_in(rng, 6), dim), (blocks,), jnp.float32, least / len(pieces), top_value / len(pieces))
        factor_of = factor_of * jnp.repeat(jnp.exp(steps), dims[dim] // blocks).reshape((-1,) + (1,) * (len(dims) - 1 - dim))
    return factor_of


def routed_block(key, own, number, rows, amount, top, reach, slope):
    order = jax.random.permutation(key, amount)
    packed, common = load_shares(amount, rows * top, reach, slope, True), load_shares(amount, rows * top, reach, slope, False)
    places = jnp.arange(amount)

    def named(tallies, rotation):
        used = int((tallies > 0).sum())
        fixed = max(1, used // 4)
        passed = fixed + (places - fixed + rotation * (used - fixed)) % max(1, amount - fixed)
        return jnp.zeros((amount,), jnp.int32).at[order[jnp.where(places < fixed, places, passed)]].set(jnp.asarray(tallies, jnp.int32))

    tallies = jnp.where(number % 4 == 0, named(packed, number // 4), named(common, number - number // 4 - 1))
    mixed = jax.random.permutation(jax.random.fold_in(own, 3), amount)
    donor, sink = mixed[0:amount // 2 * 2:2], mixed[1:amount // 2 * 2:2]
    margin = jnp.minimum(tallies[donor] - 1, reach - tallies[sink]) // 2
    margin = jnp.where((donor == order[0]) | (sink == order[0]) | (tallies[sink] == 0), 0, jnp.maximum(margin, 0))
    passed = jax.random.randint(jax.random.fold_in(own, 4), (amount // 2,), 0, 1 << 20) % (margin + 1)
    tallies = tallies.at[donor].add(-passed).at[sink].add(passed)
    members = jnp.searchsorted(jnp.cumsum(tallies), jnp.arange(rows * top), side="right").astype(jnp.int32)
    grid = members.reshape(top, rows).T
    grid = grid[jax.random.permutation(jax.random.fold_in(own, 1), rows)]
    rotation = jax.random.randint(jax.random.fold_in(own, 2), (rows, 1), 0, top)
    return jnp.take_along_axis(grid, (jnp.arange(top)[None, :] + rotation) % top, axis=1)


def load_shares(number_of, total, bound, slope, full):
    weights = [(1 << 20) // math.isqrt(rank ** slope) + 1 for rank in range(1, number_of + 1)]
    largest = bound if full else min(bound, max(-(-total // number_of), total * weights[0] // sum(weights)))
    least = 1 if total - largest >= number_of - 1 else 0
    holding, surplus = [largest] + [least] * (number_of - 1), total - largest - least * (number_of - 1)
    while surplus > 0:
        free = [i for i in range(1, number_of) if holding[i] < largest] or [i for i in range(1, number_of) if holding[i] < bound]
        pool, budget = sum([weights[i] for i in free]), surplus
        for i in free:
            addition = min(bound - holding[i], max(1, budget * weights[i] // pool), surplus)
            holding[i] = holding[i] + addition
            surplus = surplus - addition
    return np.array(holding)


def normal_values(own_key, shape, scale, bound, cuts=(), kind=jnp.bfloat16):
    drawn = jax.random.normal(own_key, shape, jnp.float32) * scale
    if len(cuts) > 0:
        drawn = block_levels(own_key, shape, cuts, -0.22, 0.18) * drawn
    return jnp.clip(drawn, min=-bound, max=bound).astype(kind)


def setup_inputs(seed: int = 0) -> dict:
    streams_of = jax.random.split(jax.random.key(seed), 9)
    tokens = normal_values(streams_of[0], (TOKENS, MODEL_WIDTH), 1.0, 6.0, ((0, 8), (1, 16)))
    gain = jnp.clip(1.0 + 0.18 * jax.random.normal(streams_of[1], (MODEL_WIDTH,), jnp.float32), 0.1, 1.9)
    base_projection_weight = normal_values(streams_of[2], (MODEL_WIDTH, MODEL_WIDTH), MODEL_WIDTH ** -0.5, 0.078125, ((1, 16),))
    adapter_down_weight = normal_values(streams_of[3], (ADAPTER_TOTAL, ADAPTER_RANK, MODEL_WIDTH), MODEL_WIDTH ** -0.5, 0.078125, ((0, 8), (2, 16)))
    adapter_up_weight = normal_values(streams_of[4], (ADAPTER_TOTAL, ADAPTER_RANK, MODEL_WIDTH), ADAPTER_RANK ** -0.5, 0.75, ((0, 8), (2, 16)))
    plan = draw_plan(jax.random.fold_in(streams_of[8], 71), 0)
    target_keys = jax.random.split(jax.random.fold_in(streams_of[6], 1), TOKENS // TOK_GRP)
    target_turns = jax.random.permutation(jax.random.fold_in(streams_of[6], 3), TOKENS // TOK_GRP)
    target = jax.vmap(lambda own, number: routed_block(jax.random.fold_in(streams_of[6], 2), own, number, TOK_GRP, N_STORE, 1, CAP, 2))(target_keys, target_turns).reshape((TOKENS, 1))
    slot = plant(jax.random.randint(streams_of[7], (TOKENS,), 0, SLOTS), jax.random.fold_in(streams_of[7], 1), 0, SLOTS - 1).astype(jnp.int32)
    return dict(tokens=tokens, gain=gain, base_projection_weight=base_projection_weight, adapter_down_weight=adapter_down_weight, adapter_up_weight=adapter_up_weight, plan=plan, target=target, slot=slot)


adapter_scale = 0.5

def reference(tokens, gain, base_projection_weight, adapter_down_weight, adapter_up_weight, plan, target, slot):
    target_group = target[:, 0].astype(jnp.int32)
    copy_index = jnp.clip(slot - ADP_GRP, 0, REPL - 1).astype(jnp.int32)
    adapter = jnp.where(slot < ADP_GRP, target_group * ADP_GRP + slot, plan[target_group, copy_index]).astype(jnp.int32)
    state = tokens
    for step in range(STEPS):
        values = state.astype(jnp.float32)
        mean_sq = lax.optimization_barrier(jnp.mean(values * values, axis=1, keepdims=True))
        normed = (values * lax.rsqrt(mean_sq + 1e-05) * gain.astype(jnp.float32)[None, :]).astype(jnp.bfloat16)
        base = jnp.dot(normed, base_projection_weight, preferred_element_type=jnp.float32)

        def block_work(pair):
            rows, selected_adapter = pair
            input_factor = adapter_down_weight[selected_adapter].astype(jnp.float32)
            inner = jnp.einsum('tk,trk->tr', rows.astype(jnp.float32), input_factor).astype(jnp.bfloat16)
            output_factor = adapter_up_weight[selected_adapter].astype(jnp.float32)
            outer = jnp.einsum('tr,trk->tk', inner.astype(jnp.float32), output_factor)
            return (adapter_scale * outer).astype(jnp.bfloat16)
        delta = lax.map(block_work, (normed.reshape(-1, CAP, MODEL_WIDTH), adapter.reshape(-1, CAP))).reshape(TOKENS, MODEL_WIDTH)
        state = (values + base + delta.astype(jnp.float32)).astype(jnp.bfloat16)
    return state
```

```python
import functools

import jax
import jax.numpy as jnp
from jax import lax
from jax.experimental import pallas as pl
from jax.experimental.pallas import tpu as pltpu
from jax.sharding import PartitionSpec as P

MESH = pl.DeviceIdType.MESH
STEPS = 4
SCALE = 0.5
EPS = 1e-05
HOPS = (2, 1, 3)
BF = jnp.bfloat16
F32 = jnp.float32


def kernel(
    parts, tok, gain, w, down, up, plan, tgt, slt, out,
    w2, dn, un, acts, ext, sbuf, rbuf, own, xown, state, ids,
    w_send, w_recv, w_loc, a_send, a_recv, a_loc, g_send, g_recv, r_send, r_recv,
):
    rows_all, width = tok.shape
    rows = rows_all // parts
    slots = down.shape[0]
    half = slots // 2
    features = gain.shape[1]
    s = lax.axis_index("store")
    m = lax.axis_index("mp")
    z, c = s // 2, s % 2
    y, x = m // 4, m % 4
    p = x * (1 - c) + y * c
    q = y * (1 - c) + x * c

    def mp_of(pp, qq):
        return (qq * 4 + pp) * (1 - c) + (pp * 4 + qq) * c

    def p_peer(k):
        return (s, mp_of((p + k) % 4, q))

    def q_peer(k):
        return (s, mp_of(p, (q + k) % 4))

    def z_peer(k):
        return (((z + k) % 4) * 2 + c, m)

    mate = (z * 2 + 1 - c, m)

    def remote(src, dst, send, recv, device):
        return pltpu.make_async_remote_copy(
            src_ref=src, dst_ref=dst, send_sem=send, recv_sem=recv,
            device_id=device, device_id_type=MESH,
        )

    barrier = pltpu.get_barrier_semaphore()
    for k in HOPS:
        pl.semaphore_signal(barrier, inc=1, device_id=p_peer(k), device_id_type=MESH)
        pl.semaphore_signal(barrier, inc=1, device_id=q_peer(k), device_id_type=MESH)
    for k in (1, 3):
        pl.semaphore_signal(barrier, inc=1, device_id=z_peer(k), device_id_type=MESH)
    pl.semaphore_signal(barrier, inc=1, device_id=mate, device_id_type=MESH)
    pl.semaphore_wait(barrier, 9)

    lo, hi = pl.ds(0, half), pl.ds(half, half)
    s_left, s_right, s_far = ((z + 3) % 4) * 2 + c, ((z + 1) % 4) * 2 + c, ((z + 2) % 4) * 2 + c

    def adapter_copies(f, src, dst):
        def go(i, a, b, device):
            return remote(a, b, a_send.at[f, i], a_recv.at[f, i], device)

        here = [
            go(0, src.at[lo], dst.at[s, lo], z_peer(1)),
            go(1, src.at[hi], dst.at[s, hi], z_peer(1)),
            go(2, src.at[hi], dst.at[s, hi], z_peer(3)),
            go(3, src.at[lo], dst.at[s, lo], z_peer(3)),
            go(4, src, dst.at[s], mate),
        ]
        on = [
            go(5, dst.at[s_left, lo], dst.at[s_left, lo], z_peer(1)),
            go(6, dst.at[s_right, hi], dst.at[s_right, hi], z_peer(3)),
        ]
        across = [
            go(7 + i, dst.at[o, part], dst.at[o, part], mate)
            for i, (o, part) in enumerate(
                ((s_left, lo), (s_right, hi), (s_left, hi), (s_right, lo), (s_far, lo), (s_far, hi))
            )
        ]
        keep = pltpu.make_async_copy(src, dst.at[s], a_loc.at[f])
        return here, on, across, keep

    d_here, d_on, d_across, d_keep = adapter_copies(0, down, dn)
    u_here, u_on, u_across, u_keep = adapter_copies(1, up, un)

    def begin(here, keep):
        for i in (0, 2, 1, 3, 4):
            here[i].start()
        keep.start()

    begin(d_here, d_keep)

    w_out = []
    for i, k in enumerate(HOPS):
        for j in range(4):
            first = pl.multiple_of(mp_of((p + j) % 4, (q + k) % 4) * width, 128)
            w_out.append(
                remote(
                    w.at[pl.ds(first, width)], w2.at[4 - k, pl.ds(j * width, width)],
                    w_send.at[i, j], w_recv.at[i, j], q_peer(k),
                )
            )
    w_keep = []
    for j in range(4):
        first = pl.multiple_of(mp_of((p + j) % 4, q) * width, 128)
        w_keep.append(
            pltpu.make_async_copy(
                w.at[pl.ds(first, width)], w2.at[0, pl.ds(j * width, width)], w_loc.at[j]
            )
        )

    lane = lax.broadcasted_iota(jnp.int32, (rows, 128), 1)
    low = lane < 64

    def act_copies(h, par):
        return [
            remote(
                acts.at[h, par, :, pl.ds(0, width)],
                acts.at[h, par, :, pl.ds((4 - k) * width, width)],
                g_send.at[h, par, i], g_recv.at[h, par, i], p_peer(k),
            )
            for i, k in enumerate(HOPS)
        ]

    def ext_copies(h, par):
        return [
            remote(
                ext.at[h, par, 0], ext.at[h, par, 4 - k],
                g_send.at[h, par, 3 + i], g_recv.at[h, par, 3 + i], p_peer(k),
            )
            for i, k in enumerate(HOPS)
        ]

    def sum_copies(h, par):
        return [
            remote(
                sbuf.at[h, par, i], rbuf.at[h, par, i],
                r_send.at[h, par, i], r_recv.at[h, par, i], q_peer(k),
            )
            for i, k in enumerate(HOPS)
        ]

    gain_here = gain[:, pl.ds(pl.multiple_of(m * width, 128), width)]

    def send_scaled(h, par):
        now = state[h].astype(F32)
        acts[h, par, :, 0:width] = (now * gain_here).astype(BF)
        for cp in act_copies(h, par):
            cp.start()

    def split(total):
        top = total.astype(BF).astype(F32)
        return top, total - top

    def send_inner(h, par):
        now = state[h].astype(F32)
        square = jnp.sum(now * now, axis=1, keepdims=True)
        mine = acts[h, par, :, 0:width]
        who = ids[h]
        acc = jnp.zeros((rows, 128), F32)
        for g in range(8):
            part = lax.dot_general(
                mine, dn[g], (((1,), (1,)), ((), ())), preferred_element_type=F32
            )
            for t in range(4):
                acc += jnp.where(who == g * 8 + 2 * t, part[:, t * 128:(t + 1) * 128], 0.0)
        acc += pltpu.roll(acc, 64, 1)
        top, rest = split(square)
        ext[h, par, 0] = jnp.where(low, acc, jnp.where(lane == 64, top, rest)).astype(BF)
        for cp in ext_copies(h, par):
            cp.start()

    def multiply(h, par):
        for cp in act_copies(h, par) + ext_copies(h, par):
            cp.wait()
        both = ext[h, par, 0].astype(F32)
        for i in range(1, 4):
            both += ext[h, par, i].astype(F32)
        square = both[:, 64:65] + both[:, 65:66]
        top, rest = split(square)
        extra = jnp.where(low, both, jnp.where(lane == 64, top, rest)).astype(BF)
        xown[h] = jnp.where(low, both, square)
        copies = sum_copies(h, par)
        for i, k in enumerate(HOPS):
            part = jnp.dot(acts[h, par], w2[k], preferred_element_type=F32)
            sbuf[h, par, i, :, 0:width] = part.astype(BF)
            sbuf[h, par, i, :, width:width + 128] = extra
            copies[i].start()
        own[h] = jnp.dot(acts[h, par], w2[0], preferred_element_type=F32)

    def finish(h, par):
        for cp in sum_copies(h, par):
            cp.wait()
        base = own[h]
        both = jnp.zeros((rows, 128), F32)
        for i in range(3):
            base += rbuf[h, par, i, :, 0:width].astype(F32)
            both += rbuf[h, par, i, :, width:width + 128].astype(F32)
        mine = xown[h]
        square = both[:, 64:65] + both[:, 65:66] + mine[:, 64:65]
        scale = lax.rsqrt(square * (1.0 / features) + EPS)
        inner = jnp.where(low, (both + mine) * scale, 0.0)
        inner = (inner + pltpu.roll(inner, 64, 1)).astype(BF).astype(F32)
        who = ids[h]
        outer = jnp.zeros((rows, width), F32)
        for g in range(8):
            spread = jnp.concatenate(
                [jnp.where(who == g * 8 + 2 * t, inner, 0.0).astype(BF) for t in range(4)], axis=1
            )
            outer += jnp.dot(spread, un[g], preferred_element_type=F32)
        delta = (SCALE * outer).astype(BF).astype(F32)
        state[h] = (state[h].astype(F32) + base * scale + delta).astype(BF)

    for h in range(parts):
        state[h] = tok[h * rows:(h + 1) * rows]

    @pl.loop(0, parts)
    def _(h):
        send_scaled(h, 0)

    for j in range(4):
        for i in range(3):
            w_out[i * 4 + j].start()
    for cp in w_keep:
        cp.start()

    for h in range(parts):
        group = jnp.broadcast_to(tgt[h * rows:(h + 1) * rows], (rows, 128))
        place = jnp.broadcast_to(slt[h * rows:(h + 1) * rows], (rows, 128))
        key = group * 4 + place - 8
        chosen = group * 8 + place
        for g in range(8):
            for r in range(4):
                hit = jnp.logical_and(place >= 8, key == g * 4 + r)
                chosen = jnp.where(hit, plan[g, r], chosen)
        ids[h] = chosen - jnp.where(low, 0, 1)

    def pass_on(here, on, across):
        here[0].wait_recv()
        on[0].start()
        across[0].start()
        here[2].wait_recv()
        on[1].start()
        across[1].start()

    def pass_rest(here, across):
        here[1].wait_recv()
        across[2].start()
        here[3].wait_recv()
        across[3].start()

    def pass_last(on, across):
        on[0].wait_recv()
        across[4].start()
        on[1].wait_recv()
        across[5].start()

    def settle(here, on, across, keep):
        here[4].wait_recv()
        keep.wait()
        for cp in across:
            cp.wait_recv()

    def drain(here, on, across):
        for cp in here + on + across:
            cp.wait_send()

    pass_on(d_here, d_on, d_across)
    begin(u_here, u_keep)
    pass_rest(d_here, d_across)
    pass_last(d_on, d_across)
    settle(d_here, d_on, d_across, d_keep)

    @pl.loop(0, parts)
    def _(h):
        send_inner(h, 0)

    pass_on(u_here, u_on, u_across)
    pass_rest(u_here, u_across)
    for cp in w_keep:
        cp.wait()
    for cp in w_out:
        cp.wait()

    def step(t):
        par = t % 2

        @pl.loop(0, parts)
        def _(h):
            multiply(h, par)

        @pl.when(t == 0)
        def _():
            pass_last(u_on, u_across)
            settle(u_here, u_on, u_across, u_keep)

        @pl.loop(0, parts)
        def _(h):
            finish(h, par)

            @pl.when(t < STEPS - 1)
            def _():
                send_scaled(h, 1 - par)
                send_inner(h, 1 - par)

    @pl.loop(0, STEPS)
    def _(t):
        step(t)

    drain(d_here, d_on, d_across)
    drain(u_here, u_on, u_across)
    for h in range(parts):
        out[h * rows:(h + 1) * rows] = state[h]


PARTS = 2


def local(tokens, gain, base_weight, down, up, plan, target, slot):
    rows_all, width = tokens.shape
    owned, rank, _ = down.shape
    stores = 8
    rows = rows_all // PARTS
    dma = pltpu.SemaphoreType.DMA
    vmem = pl.BlockSpec(memory_space=pltpu.VMEM)
    anywhere = pl.BlockSpec(memory_space=pl.ANY)
    return pl.pallas_call(
        functools.partial(kernel, PARTS),
        out_shape=jax.ShapeDtypeStruct((rows_all, width), BF),
        in_specs=[
            vmem, vmem, anywhere, anywhere, anywhere,
            pl.BlockSpec(memory_space=pltpu.SMEM), vmem, vmem,
        ],
        out_specs=vmem,
        scratch_shapes=[
            pltpu.VMEM((4, 4 * width, width), BF),
            pltpu.VMEM((stores, owned * rank, width), BF),
            pltpu.VMEM((stores, owned * rank, width), BF),
            pltpu.VMEM((PARTS, 2, rows, 4 * width), BF),
            pltpu.VMEM((PARTS, 2, 4, rows, 128), BF),
            pltpu.VMEM((PARTS, 2, 3, rows, width + 128), BF),
            pltpu.VMEM((PARTS, 2, 3, rows, width + 128), BF),
            pltpu.VMEM((PARTS, rows, width), F32),
            pltpu.VMEM((PARTS, rows, 128), F32),
            pltpu.VMEM((PARTS, rows, width), BF),
            pltpu.VMEM((PARTS, rows, 128), jnp.int32),
            dma((3, 4)), dma((3, 4)), dma((4,)),
            dma((2, 13)), dma((2, 13)), dma((2,)),
            dma((PARTS, 2, 6)), dma((PARTS, 2, 6)),
            dma((PARTS, 2, 3)), dma((PARTS, 2, 3)),
        ],
        compiler_params=pltpu.CompilerParams(
            collective_id=0, has_side_effects=True, vmem_limit_bytes=56 << 20
        ),
    )(
        tokens, gain.reshape(1, -1), base_weight,
        down.reshape(owned * rank, width), up.reshape(owned * rank, width),
        plan, target, slot.reshape(-1, 1),
    )


def solution(mesh):
    return jax.shard_map(
        local,
        mesh=mesh,
        in_specs=(
            P("store", "mp"),
            P(),
            P(None, "mp"),
            P("store", None, "mp"),
            P("store", None, "mp"),
            P(),
            P("store", None),
            P("store"),
        ),
        out_specs=P("store", "mp"),
        check_vma=False,
    )
```

```python
import functools

import jax
import jax.numpy as jnp
from jax import lax
from jax.experimental import pallas as pl
from jax.experimental.pallas import tpu as pltpu
from jax.sharding import PartitionSpec as P

MESH = pl.DeviceIdType.MESH
STEPS = 4
SCALE = 0.5
EPS = 1e-05
HOPS = (1, 3, 2)
PLACE = {1: 0, 3: 1, 2: 2, 0: 3}
BF = jnp.bfloat16
F32 = jnp.float32


def kernel(
    parts, groups, tok, gain, w, down, up, plan, tgt, slt, out,
    w2, dn, un, acts, ext, sbuf, rbuf, xbuf, xrec, own, xown, sown, delta, scale, state, ids,
    w_send, w_recv, w_loc, a_send, a_recv, a_loc,
    g_send, g_recv, e_send, e_recv, r_send, r_recv, x_send, x_recv,
):
    rows_all, width = tok.shape
    rows = rows_all // parts
    block = rows_all // groups
    deep = block // 2
    slots = down.shape[0]
    half = slots // 2
    features = gain.shape[1]
    s = lax.axis_index("store")
    m = lax.axis_index("mp")
    z, c = s // 2, s % 2
    y, x = m // 4, m % 4
    p = x * (1 - c) + y * c
    q = y * (1 - c) + x * c

    def mp_of(pp, qq):
        return (qq * 4 + pp) * (1 - c) + (pp * 4 + qq) * c

    def p_peer(k):
        return (s, mp_of((p + k) % 4, q))

    def q_peer(k):
        return (s, mp_of(p, (q + k) % 4))

    def z_peer(k):
        return (((z + k) % 4) * 2 + c, m)

    mate = (z * 2 + 1 - c, m)

    def remote(src, dst, send, recv, device):
        return pltpu.make_async_remote_copy(
            src_ref=src, dst_ref=dst, send_sem=send, recv_sem=recv,
            device_id=device, device_id_type=MESH,
        )

    barrier = pltpu.get_barrier_semaphore()
    for k in HOPS:
        pl.semaphore_signal(barrier, inc=1, device_id=p_peer(k), device_id_type=MESH)
        pl.semaphore_signal(barrier, inc=1, device_id=q_peer(k), device_id_type=MESH)
    for k in (1, 3):
        pl.semaphore_signal(barrier, inc=1, device_id=z_peer(k), device_id_type=MESH)
    pl.semaphore_signal(barrier, inc=1, device_id=mate, device_id_type=MESH)
    pl.semaphore_wait(barrier, 9)

    lo, hi = pl.ds(0, half), pl.ds(half, half)
    s_left, s_right, s_far = ((z + 3) % 4) * 2 + c, ((z + 1) % 4) * 2 + c, ((z + 2) % 4) * 2 + c

    def adapter_copies(f, src, dst):
        def go(i, a, b, device):
            return remote(a, b, a_send.at[f, i], a_recv.at[f, i], device)

        here = [
            go(0, src.at[lo], dst.at[s, lo], z_peer(1)),
            go(1, src.at[hi], dst.at[s, hi], z_peer(1)),
            go(2, src.at[hi], dst.at[s, hi], z_peer(3)),
            go(3, src.at[lo], dst.at[s, lo], z_peer(3)),
            go(4, src, dst.at[s], mate),
        ]
        on = [
            go(5, dst.at[s_left, lo], dst.at[s_left, lo], z_peer(1)),
            go(6, dst.at[s_right, hi], dst.at[s_right, hi], z_peer(3)),
        ]
        across = [
            go(7 + i, dst.at[o, part], dst.at[o, part], mate)
            for i, (o, part) in enumerate(
                ((s_left, lo), (s_right, hi), (s_left, hi), (s_right, lo), (s_far, lo), (s_far, hi))
            )
        ]
        keep = pltpu.make_async_copy(src, dst.at[s], a_loc.at[f])
        return here, on, across, keep

    d_here, d_on, d_across, d_keep = adapter_copies(0, down, dn)
    u_here, u_on, u_across, u_keep = adapter_copies(1, up, un)

    def begin(here, keep):
        for i in (0, 2, 1, 3, 4):
            here[i].start()
        keep.start()

    begin(d_here, d_keep)

    w_out = []
    for i, k in enumerate(HOPS):
        for j in range(4):
            first = pl.multiple_of(mp_of((p + j) % 4, (q + k) % 4) * width, 128)
            w_out.append(
                remote(
                    w.at[pl.ds(first, width)],
                    w2.at[pl.ds(j * width, width), pl.ds(PLACE[4 - k] * width, width)],
                    w_send.at[i, j], w_recv.at[i, j], q_peer(k),
                )
            )
    w_keep = []
    for j in range(4):
        first = pl.multiple_of(mp_of((p + j) % 4, q) * width, 128)
        w_keep.append(
            pltpu.make_async_copy(
                w.at[pl.ds(first, width)],
                w2.at[pl.ds(j * width, width), pl.ds(PLACE[0] * width, width)],
                w_loc.at[j],
            )
        )

    low = lax.broadcasted_iota(jnp.int32, (deep, 128), 1) < 64
    diagonal = lax.broadcasted_iota(jnp.int32, (block, 128), 0) == lax.broadcasted_iota(
        jnp.int32, (block, 128), 1
    )
    line = lax.broadcasted_iota(jnp.int32, (16, 128), 0)

    def part(h):
        return pl.ds(pl.multiple_of(h * rows, rows), rows)

    def group(g):
        return pl.ds(pl.multiple_of(g * block, block), block)

    def act_copies(h, par):
        return [
            remote(
                acts.at[par, part(h), pl.ds(0, width)],
                acts.at[par, part(h), pl.ds((4 - k) * width, width)],
                g_send.at[par, h, i], g_recv.at[par, h, i], p_peer(k),
            )
            for i, k in enumerate(HOPS)
        ]

    def ext_copies(g, par):
        return [
            remote(
                ext.at[par, g, 0], ext.at[par, g, 4 - k],
                e_send.at[par, g, i], e_recv.at[par, g, i], p_peer(k),
            )
            for i, k in enumerate(HOPS)
        ]

    def sum_copies(h, par):
        return [
            remote(
                sbuf.at[par, i, part(h)], rbuf.at[par, i, part(h)],
                r_send.at[par, h, i], r_recv.at[par, h, i], q_peer(k),
            )
            for i, k in enumerate(HOPS)
        ]

    def inner_copies(g, par):
        return [
            remote(
                xbuf.at[par, g], xrec.at[par, g, i],
                x_send.at[par, g, i], x_recv.at[par, g, i], q_peer(k),
            )
            for i, k in enumerate(HOPS)
        ]

    gain_here = gain[:, pl.ds(pl.multiple_of(m * width, 128), width)]

    def send_scaled(h, par):
        acts[par, part(h), 0:width] = (state[part(h)].astype(F32) * gain_here).astype(BF)
        for cp in act_copies(h, par):
            cp.start()

    def as_column(row):
        return jnp.sum(jnp.where(diagonal, row, 0.0), axis=1, keepdims=True)

    def packed(inner, square):
        top = square.astype(BF).astype(F32)
        tail = jnp.where(line == 0, top, jnp.where(line == 1, square - top, 0.0))
        return inner.astype(BF), tail.astype(BF)

    def send_inner(g, par):
        now = state[group(g)].astype(F32)
        square = jnp.sum(now * now, axis=1, keepdims=True)
        square = jnp.sum(jnp.where(diagonal, square, 0.0), axis=0, keepdims=True)
        mine = acts[par, group(g), 0:width]
        who = ids[group(g)]
        acc = jnp.zeros((block, 128), F32)
        for a in range(8):
            value = lax.dot_general(
                mine, dn[a], (((1,), (1,)), ((), ())), preferred_element_type=F32
            )
            for t in range(4):
                acc += jnp.where(
                    who == float(a * 8 + 2 * t), value[:, t * 128:(t + 1) * 128], 0.0
                )
        acc += pltpu.roll(acc, 64, 1)
        body, tail = packed(jnp.where(low, acc[:deep], acc[deep:]), square)
        ext[par, g, 0, 0:deep] = body
        ext[par, g, 0, deep:deep + 16] = tail
        for cp in ext_copies(g, par):
            cp.start()

    def multiply(h, par):
        for cp in act_copies(h, par):
            cp.wait()
        copies = sum_copies(h, par)
        left = acts[par, part(h)]
        value = jnp.dot(left, w2[:, 0:2 * width], preferred_element_type=F32).astype(BF)
        sbuf[par, 0, part(h)] = value[:, :width]
        copies[0].start()
        sbuf[par, 1, part(h)] = value[:, width:]
        copies[1].start()
        value = jnp.dot(left, w2[:, 2 * width:4 * width], preferred_element_type=F32)
        sbuf[par, 2, part(h)] = value[:, :width].astype(BF)
        copies[2].start()
        own[part(h)] = value[:, width:]

    def forward(g, par):
        for cp in ext_copies(g, par):
            cp.wait()
        both = ext[par, g, 0].astype(F32)
        for i in range(1, 4):
            both += ext[par, g, i].astype(F32)
        inner, square = both[:deep], both[deep:deep + 1] + both[deep + 1:deep + 2]
        body, tail = packed(inner, square)
        xbuf[par, g, 0:deep] = body
        xbuf[par, g, deep:deep + 16] = tail
        for cp in inner_copies(g, par):
            cp.start()
        xown[g] = inner
        sown[g] = jnp.broadcast_to(square, (8, 128))

    def adapt(g, par):
        for cp in inner_copies(g, par):
            cp.wait()
        both = xrec[par, g, 0].astype(F32)
        for i in range(1, 3):
            both += xrec[par, g, i].astype(F32)
        square = both[deep:deep + 1] + both[deep + 1:deep + 2] + sown[g, 0:1]
        factor = as_column(lax.rsqrt(square * (1.0 / features) + EPS))
        scale[group(g)] = jnp.broadcast_to(factor, (block, 128))
        inner = both[:deep] + xown[g]
        other = pltpu.roll(inner, 64, 1)
        inner = jnp.concatenate([jnp.where(low, inner, other), jnp.where(low, other, inner)], 0)
        inner = (inner * factor).astype(BF).astype(F32)
        who = ids[group(g)]
        outer = jnp.zeros((block, width), F32)
        for a in range(8):
            spread = jnp.concatenate(
                [
                    jnp.where(who == float(a * 8 + 2 * t), inner, 0.0).astype(BF)
                    for t in range(4)
                ],
                axis=1,
            )
            outer += jnp.dot(spread, un[a], preferred_element_type=F32)
        delta[group(g)] = (SCALE * outer).astype(BF)

    def finish(h, par):
        for cp in sum_copies(h, par):
            cp.wait()
        base = own[part(h)]
        for i in range(3):
            base += rbuf[par, i, part(h)].astype(F32)
        factor = jnp.concatenate([scale[part(h)]] * (width // 128), axis=1)
        now = state[part(h)].astype(F32) + base * factor + delta[part(h)].astype(F32)
        state[part(h)] = now.astype(BF)

    state[...] = tok[...]

    @pl.loop(0, parts)
    def _(h):
        send_scaled(h, 0)

    for j in range(4):
        for i in range(3):
            w_out[i * 4 + j].start()
    for cp in w_keep:
        cp.start()

    wanted = tgt[...]
    place = slt[...]
    key = wanted * 4 + place - 8
    chosen = wanted * 8 + place
    for a in range(8):
        for r in range(4):
            hit = jnp.logical_and(place >= 8, key == a * 4 + r)
            chosen = jnp.where(hit, plan[r, a], chosen)
    chosen = chosen.astype(F32)
    upper = (lax.broadcasted_iota(jnp.int32, (block, 128), 1) >= 64).astype(F32)
    for g in range(groups):
        ids[g * block:(g + 1) * block] = as_column(chosen[:, g * block:(g + 1) * block]) - upper

    def pass_on(here, on, across):
        here[0].wait_recv()
        on[0].start()
        across[0].start()
        here[2].wait_recv()
        on[1].start()
        across[1].start()

    def pass_rest(here, across):
        here[1].wait_recv()
        across[2].start()
        here[3].wait_recv()
        across[3].start()

    def pass_last(on, across):
        on[0].wait_recv()
        across[4].start()
        on[1].wait_recv()
        across[5].start()

    def settle(here, across, keep):
        here[4].wait_recv()
        keep.wait()
        for cp in across:
            cp.wait_recv()

    def drain(here, on, across):
        for cp in here + on + across:
            cp.wait_send()

    pass_on(d_here, d_on, d_across)
    begin(u_here, u_keep)
    pass_rest(d_here, d_across)
    pass_last(d_on, d_across)
    settle(d_here, d_across, d_keep)

    @pl.loop(0, groups)
    def _(g):
        send_inner(g, 0)

    pass_on(u_here, u_on, u_across)
    pass_rest(u_here, u_across)
    for cp in w_keep:
        cp.wait()
    for cp in w_out:
        cp.wait()

    per = parts // groups

    @pl.loop(0, STEPS)
    def _(t):
        par = t % 2

        @pl.loop(0, groups)
        def _(g):
            multiply(g * per, par)
            forward(g, par)
            for i in range(1, per):
                multiply(g * per + i, par)

        @pl.when(t == 0)
        def _():
            pass_last(u_on, u_across)
            settle(u_here, u_across, u_keep)

        @pl.loop(0, groups)
        def _(g):
            adapt(g, par)

            @pl.loop(0, per)
            def _(i):
                h = g * per + i
                finish(h, par)

                @pl.when(t < STEPS - 1)
                def _():
                    send_scaled(h, 1 - par)

            @pl.when(t < STEPS - 1)
            def _():
                send_inner(g, 1 - par)

    drain(d_here, d_on, d_across)
    drain(u_here, u_on, u_across)
    out[...] = state[...]


PARTS = 4
GROUPS = 2


def local(tokens, gain, base_weight, down, up, plan, target, slot):
    rows_all, width = tokens.shape
    owned, rank, _ = down.shape
    stores = 8
    lines = rows_all // GROUPS // 2 + 16
    dma = pltpu.SemaphoreType.DMA
    vmem = pl.BlockSpec(memory_space=pltpu.VMEM)
    anywhere = pl.BlockSpec(memory_space=pl.ANY)
    return pl.pallas_call(
        functools.partial(kernel, PARTS, GROUPS),
        out_shape=jax.ShapeDtypeStruct((rows_all, width), BF),
        in_specs=[
            vmem, vmem, anywhere, anywhere, anywhere,
            pl.BlockSpec(memory_space=pltpu.SMEM), vmem, vmem,
        ],
        out_specs=vmem,
        scratch_shapes=[
            pltpu.VMEM((4 * width, 4 * width), BF),
            pltpu.VMEM((stores, owned * rank, width), BF),
            pltpu.VMEM((stores, owned * rank, width), BF),
            pltpu.VMEM((2, rows_all, 4 * width), BF),
            pltpu.VMEM((2, GROUPS, 4, lines, 128), BF),
            pltpu.VMEM((2, 3, rows_all, width), BF),
            pltpu.VMEM((2, 3, rows_all, width), BF),
            pltpu.VMEM((2, GROUPS, lines, 128), BF),
            pltpu.VMEM((2, GROUPS, 3, lines, 128), BF),
            pltpu.VMEM((rows_all, width), F32),
            pltpu.VMEM((GROUPS, lines - 16, 128), F32),
            pltpu.VMEM((GROUPS, 8, 128), F32),
            pltpu.VMEM((rows_all, width), BF),
            pltpu.VMEM((rows_all, 128), F32),
            pltpu.VMEM((rows_all, width), BF),
            pltpu.VMEM((rows_all, 128), F32),
            dma((3, 4)), dma((3, 4)), dma((4,)),
            dma((2, 13)), dma((2, 13)), dma((2,)),
            dma((2, PARTS, 3)), dma((2, PARTS, 3)),
            dma((2, GROUPS, 3)), dma((2, GROUPS, 3)),
            dma((2, PARTS, 3)), dma((2, PARTS, 3)),
            dma((2, GROUPS, 3)), dma((2, GROUPS, 3)),
        ],
        compiler_params=pltpu.CompilerParams(
            collective_id=0, has_side_effects=True, vmem_limit_bytes=56 << 20
        ),
    )(
        tokens, gain.reshape(1, -1), base_weight,
        down.reshape(owned * rank, width), up.reshape(owned * rank, width),
        plan.T, target.reshape(1, -1), slot.reshape(1, -1),
    )


def solution(mesh):
    return jax.shard_map(
        local,
        mesh=mesh,
        in_specs=(
            P("store", "mp"),
            P(),
            P(None, "mp"),
            P("store", None, "mp"),
            P("store", None, "mp"),
            P(),
            P("store", None),
            P("store"),
        ),
        out_specs=P("store", "mp"),
        check_vma=False,
    )
```

```python
import functools

import jax
import jax.numpy as jnp
from jax import lax
from jax.experimental import pallas as pl
from jax.experimental.pallas import tpu as pltpu
from jax.sharding import PartitionSpec as P

MESH = pl.DeviceIdType.MESH
STEPS = 4
SCALE = 0.5
EPS = 1e-05
HOPS = (1, 3, 2)
PLACE = {1: 0, 3: 1, 2: 2, 0: 3}
BF = jnp.bfloat16
F32 = jnp.float32


def kernel(
    parts, groups, tok, gain, w, down, up, plan, tgt, slt, out,
    w2, dn, un, acts, ext, sbuf, rbuf, xbuf, xrec, own, xown, sown, delta, scale, state, ids,
    w_send, w_recv, w_loc, a_send, a_recv, a_loc,
    g_send, g_recv, e_send, e_recv, r_send, r_recv, x_send, x_recv, pair,
):
    rows_all, width = tok.shape
    rows = rows_all // parts
    block = rows_all // groups
    deep = block // 2
    slots = down.shape[0]
    half = slots // 2
    features = gain.shape[1]
    s = lax.axis_index("store")
    m = lax.axis_index("mp")
    z, c = s // 2, s % 2
    y, x = m // 4, m % 4
    p = x * (1 - c) + y * c
    q = y * (1 - c) + x * c

    def mp_of(pp, qq):
        return (qq * 4 + pp) * (1 - c) + (pp * 4 + qq) * c

    def p_peer(k):
        return (s, mp_of((p + k) % 4, q))

    def q_peer(k):
        return (s, mp_of(p, (q + k) % 4))

    def z_peer(k):
        return (((z + k) % 4) * 2 + c, m)

    mate = (z * 2 + 1 - c, m)

    def remote(src, dst, send, recv, device):
        return pltpu.make_async_remote_copy(
            src_ref=src, dst_ref=dst, send_sem=send, recv_sem=recv,
            device_id=device, device_id_type=MESH,
        )

    barrier = pltpu.get_barrier_semaphore()
    for k in HOPS:
        pl.semaphore_signal(barrier, inc=1, device_id=p_peer(k), device_id_type=MESH)
        pl.semaphore_signal(barrier, inc=1, device_id=q_peer(k), device_id_type=MESH)
    for k in (1, 3):
        pl.semaphore_signal(barrier, inc=1, device_id=z_peer(k), device_id_type=MESH)
    pl.semaphore_signal(barrier, inc=1, device_id=mate, device_id_type=MESH)
    pl.semaphore_wait(barrier, 9)

    lo, hi = pl.ds(0, half), pl.ds(half, half)
    s_left, s_right, s_far = ((z + 3) % 4) * 2 + c, ((z + 1) % 4) * 2 + c, ((z + 2) % 4) * 2 + c

    def adapter_copies(f, src, dst):
        def go(i, a, b, device):
            return remote(a, b, a_send.at[f, i], a_recv.at[f, i], device)

        here = [
            go(0, src.at[lo], dst.at[s, lo], z_peer(1)),
            go(1, src.at[hi], dst.at[s, hi], z_peer(1)),
            go(2, src.at[hi], dst.at[s, hi], z_peer(3)),
            go(3, src.at[lo], dst.at[s, lo], z_peer(3)),
            go(4, src, dst.at[s], mate),
        ]
        on = [
            go(5, dst.at[s_left, lo], dst.at[s_left, lo], z_peer(1)),
            go(6, dst.at[s_right, hi], dst.at[s_right, hi], z_peer(3)),
        ]
        across = [
            go(7 + i, dst.at[o, part], dst.at[o, part], mate)
            for i, (o, part) in enumerate(
                ((s_left, lo), (s_right, hi), (s_left, hi), (s_right, lo), (s_far, lo), (s_far, hi))
            )
        ]
        keep = pltpu.make_async_copy(src, dst.at[s], a_loc.at[f])
        return here, on, across, keep

    d_here, d_on, d_across, d_keep = adapter_copies(0, down, dn)
    u_here, u_on, u_across, u_keep = adapter_copies(1, up, un)

    def begin(here, keep):
        for i in (0, 2, 1, 3, 4):
            here[i].start()
        keep.start()

    begin(d_here, d_keep)

    w_out = []
    for i, k in enumerate(HOPS):
        for j in range(4):
            first = pl.multiple_of(mp_of((p + j) % 4, (q + k) % 4) * width, 128)
            w_out.append(
                remote(
                    w.at[pl.ds(first, width)],
                    w2.at[pl.ds(j * width, width), pl.ds(PLACE[4 - k] * width, width)],
                    w_send.at[i, j], w_recv.at[i, j], q_peer(k),
                )
            )
    w_keep = []
    for j in range(4):
        first = pl.multiple_of(mp_of((p + j) % 4, q) * width, 128)
        w_keep.append(
            pltpu.make_async_copy(
                w.at[pl.ds(first, width)],
                w2.at[pl.ds(j * width, width), pl.ds(PLACE[0] * width, width)],
                w_loc.at[j],
            )
        )

    low = lax.broadcasted_iota(jnp.int32, (deep, 128), 1) < 64
    diagonal = lax.broadcasted_iota(jnp.int32, (block, 128), 0) == lax.broadcasted_iota(
        jnp.int32, (block, 128), 1
    )
    line = lax.broadcasted_iota(jnp.int32, (16, 128), 0)

    def part(h):
        return pl.ds(pl.multiple_of(h * rows, rows), rows)

    def group(g):
        return pl.ds(pl.multiple_of(g * block, block), block)

    def act_copies(h, par):
        return [
            remote(
                acts.at[par, part(h), pl.ds(0, width)],
                acts.at[par, part(h), pl.ds((4 - k) * width, width)],
                g_send.at[par, h, i], g_recv.at[par, h, i], p_peer(k),
            )
            for i, k in enumerate(HOPS)
        ]

    def ext_copies(g, par):
        return [
            remote(
                ext.at[par, g, 0], ext.at[par, g, 4 - k],
                e_send.at[par, g, i], e_recv.at[par, g, i], p_peer(k),
            )
            for i, k in enumerate(HOPS)
        ]

    def sum_copies(h, par):
        return [
            remote(
                sbuf.at[par, i, part(h)], rbuf.at[par, i, part(h)],
                r_send.at[par, h, i], r_recv.at[par, h, i], q_peer(k),
            )
            for i, k in enumerate(HOPS)
        ]

    def inner_copies(g, par):
        return [
            remote(
                xbuf.at[par, g], xrec.at[par, g, i],
                x_send.at[par, g, i], x_recv.at[par, g, i], q_peer(k),
            )
            for i, k in enumerate(HOPS)
        ]

    gain_here = gain[:, pl.ds(pl.multiple_of(m * width, 128), width)]

    def send_scaled(h, par):
        acts[par, part(h), 0:width] = (state[part(h)].astype(F32) * gain_here).astype(BF)
        for cp in act_copies(h, par):
            cp.start()

    def as_column(row):
        return jnp.sum(jnp.where(diagonal, row, 0.0), axis=1, keepdims=True)

    def packed(inner, square):
        top = square.astype(BF).astype(F32)
        tail = jnp.where(line == 0, top, jnp.where(line == 1, square - top, 0.0))
        return inner.astype(BF), tail.astype(BF)

    def send_inner(g, par):
        now = state[group(g)].astype(F32)
        square = jnp.sum(now * now, axis=1, keepdims=True)
        square = jnp.sum(jnp.where(diagonal, square, 0.0), axis=0, keepdims=True)
        mine = acts[par, group(g), 0:width]
        who = ids[group(g)]
        acc = jnp.zeros((block, 128), F32)
        for a in range(8):
            value = lax.dot_general(
                mine, dn[a], (((1,), (1,)), ((), ())), preferred_element_type=F32
            )
            for t in range(4):
                acc += jnp.where(
                    who == float(a * 8 + 2 * t), value[:, t * 128:(t + 1) * 128], 0.0
                )
        acc += pltpu.roll(acc, 64, 1)
        body, tail = packed(jnp.where(low, acc[:deep], acc[deep:]), square)
        ext[par, g, 0, 0:deep] = body
        ext[par, g, 0, deep:deep + 16] = tail
        for cp in ext_copies(g, par):
            cp.start()

    def multiply(h, par):
        for cp in act_copies(h, par):
            cp.wait()
        copies = sum_copies(h, par)
        left = acts[par, part(h)]
        value = jnp.dot(left, w2[:, 0:2 * width], preferred_element_type=F32).astype(BF)
        sbuf[par, 0, part(h)] = value[:, :width]
        copies[0].start()
        sbuf[par, 1, part(h)] = value[:, width:]
        copies[1].start()
        value = jnp.dot(left, w2[:, 2 * width:4 * width], preferred_element_type=F32)
        sbuf[par, 2, part(h)] = value[:, :width].astype(BF)
        copies[2].start()
        own[part(h)] = value[:, width:]

    def forward(g, par):
        for cp in ext_copies(g, par):
            cp.wait()
        both = ext[par, g, 0].astype(F32)
        for i in range(1, 4):
            both += ext[par, g, i].astype(F32)
        inner, square = both[:deep], both[deep:deep + 1] + both[deep + 1:deep + 2]
        body, tail = packed(inner, square)
        xbuf[par, g, 0:deep] = body
        xbuf[par, g, deep:deep + 16] = tail
        for cp in inner_copies(g, par):
            cp.start()
        xown[g] = inner
        sown[g] = jnp.broadcast_to(square, (8, 128))

    def adapt(g, par):
        for cp in inner_copies(g, par):
            cp.wait()
        both = xrec[par, g, 0].astype(F32)
        for i in range(1, 3):
            both += xrec[par, g, i].astype(F32)
        square = both[deep:deep + 1] + both[deep + 1:deep + 2] + sown[g, 0:1]
        factor = as_column(lax.rsqrt(square * (1.0 / features) + EPS))
        scale[group(g)] = jnp.broadcast_to(factor, (block, 128))
        inner = both[:deep] + xown[g]
        other = pltpu.roll(inner, 64, 1)
        inner = jnp.concatenate([jnp.where(low, inner, other), jnp.where(low, other, inner)], 0)
        inner = (inner * factor).astype(BF).astype(F32)
        who = ids[group(g)]
        outer = jnp.zeros((block, width), F32)
        for a in range(8):
            spread = jnp.concatenate(
                [
                    jnp.where(who == float(a * 8 + 2 * t), inner, 0.0).astype(BF)
                    for t in range(4)
                ],
                axis=1,
            )
            outer += jnp.dot(spread, un[a], preferred_element_type=F32)
        delta[group(g)] = (SCALE * outer).astype(BF)

    def finish(h, par):
        for cp in sum_copies(h, par):
            cp.wait()
        base = own[part(h)]
        for i in range(3):
            base += rbuf[par, i, part(h)].astype(F32)
        factor = jnp.concatenate([scale[part(h)]] * (width // 128), axis=1)
        now = state[part(h)].astype(F32) + base * factor + delta[part(h)].astype(F32)
        state[part(h)] = now.astype(BF)

    state[...] = tok[...]

    @pl.loop(0, parts)
    def _(h):
        send_scaled(h, 0)

    for j in range(4):
        for i in range(3):
            w_out[i * 4 + j].start()
    for cp in w_keep:
        cp.start()

    wanted = tgt[...]
    place = slt[...]
    key = wanted * 4 + place - 8
    chosen = wanted * 8 + place
    for a in range(8):
        for r in range(4):
            hit = jnp.logical_and(place >= 8, key == a * 4 + r)
            chosen = jnp.where(hit, plan[r, a], chosen)
    chosen = chosen.astype(F32)
    upper = (lax.broadcasted_iota(jnp.int32, (block, 128), 1) >= 64).astype(F32)
    for g in range(groups):
        ids[g * block:(g + 1) * block] = as_column(chosen[:, g * block:(g + 1) * block]) - upper

    def pass_on(here, on, across):
        here[0].wait_recv()
        on[0].start()
        across[0].start()
        here[2].wait_recv()
        on[1].start()
        across[1].start()

    def pass_rest(here, across):
        here[1].wait_recv()
        across[2].start()
        here[3].wait_recv()
        across[3].start()

    def pass_last(on, across):
        on[0].wait_recv()
        across[4].start()
        on[1].wait_recv()
        across[5].start()

    def settle(here, across, keep):
        here[4].wait_recv()
        keep.wait()
        for cp in across:
            cp.wait_recv()

    def drain(here, on, across):
        for cp in here + on + across:
            cp.wait_send()

    pass_on(d_here, d_on, d_across)
    begin(u_here, u_keep)
    pass_rest(d_here, d_across)
    pass_last(d_on, d_across)
    settle(d_here, d_across, d_keep)

    @pl.loop(0, groups)
    def _(g):
        send_inner(g, 0)

    pass_on(u_here, u_on, u_across)
    pass_rest(u_here, u_across)
    for cp in w_keep:
        cp.wait()
    for cp in w_out:
        cp.wait()

    per = parts // groups

    @pl.loop(0, STEPS)
    def _(t):
        par = t % 2
        pl.semaphore_signal(pair, inc=1, device_id=mate, device_id_type=MESH)
        pl.semaphore_wait(pair, 1)

        @pl.loop(0, groups)
        def _(g):
            multiply(g * per, par)
            forward(g, par)
            for i in range(1, per):
                multiply(g * per + i, par)

        @pl.when(t == 0)
        def _():
            pass_last(u_on, u_across)
            settle(u_here, u_across, u_keep)

        @pl.loop(0, groups)
        def _(g):
            adapt(g, par)

            @pl.loop(0, per)
            def _(i):
                h = g * per + i
                finish(h, par)

                @pl.when(t < STEPS - 1)
                def _():
                    send_scaled(h, 1 - par)

            @pl.when(t < STEPS - 1)
            def _():
                send_inner(g, 1 - par)

    drain(d_here, d_on, d_across)
    drain(u_here, u_on, u_across)
    out[...] = state[...]


PARTS = 4
GROUPS = 2


def local(tokens, gain, base_weight, down, up, plan, target, slot):
    rows_all, width = tokens.shape
    owned, rank, _ = down.shape
    stores = 8
    lines = rows_all // GROUPS // 2 + 16
    dma = pltpu.SemaphoreType.DMA
    vmem = pl.BlockSpec(memory_space=pltpu.VMEM)
    anywhere = pl.BlockSpec(memory_space=pl.ANY)
    return pl.pallas_call(
        functools.partial(kernel, PARTS, GROUPS),
        out_shape=jax.ShapeDtypeStruct((rows_all, width), BF),
        in_specs=[
            vmem, vmem, anywhere, anywhere, anywhere,
            pl.BlockSpec(memory_space=pltpu.SMEM), vmem, vmem,
        ],
        out_specs=vmem,
        scratch_shapes=[
            pltpu.VMEM((4 * width, 4 * width), BF),
            pltpu.VMEM((stores, owned * rank, width), BF),
            pltpu.VMEM((stores, owned * rank, width), BF),
            pltpu.VMEM((2, rows_all, 4 * width), BF),
            pltpu.VMEM((2, GROUPS, 4, lines, 128), BF),
            pltpu.VMEM((2, 3, rows_all, width), BF),
            pltpu.VMEM((2, 3, rows_all, width), BF),
            pltpu.VMEM((2, GROUPS, lines, 128), BF),
            pltpu.VMEM((2, GROUPS, 3, lines, 128), BF),
            pltpu.VMEM((rows_all, width), F32),
            pltpu.VMEM((GROUPS, lines - 16, 128), F32),
            pltpu.VMEM((GROUPS, 8, 128), F32),
            pltpu.VMEM((rows_all, width), BF),
            pltpu.VMEM((rows_all, 128), F32),
            pltpu.VMEM((rows_all, width), BF),
            pltpu.VMEM((rows_all, 128), F32),
            dma((3, 4)), dma((3, 4)), dma((4,)),
            dma((2, 13)), dma((2, 13)), dma((2,)),
            dma((2, PARTS, 3)), dma((2, PARTS, 3)),
            dma((2, GROUPS, 3)), dma((2, GROUPS, 3)),
            dma((2, PARTS, 3)), dma((2, PARTS, 3)),
            dma((2, GROUPS, 3)), dma((2, GROUPS, 3)),
            pltpu.SemaphoreType.REGULAR,
        ],
        compiler_params=pltpu.CompilerParams(
            collective_id=0, has_side_effects=True, vmem_limit_bytes=56 << 20
        ),
    )(
        tokens, gain.reshape(1, -1), base_weight,
        down.reshape(owned * rank, width), up.reshape(owned * rank, width),
        plan.T, target.reshape(1, -1), slot.reshape(1, -1),
    )


def solution(mesh):
    return jax.shard_map(
        local,
        mesh=mesh,
        in_specs=(
            P("store", "mp"),
            P(),
            P(None, "mp"),
            P("store", None, "mp"),
            P("store", None, "mp"),
            P(),
            P("store", None),
            P("store"),
        ),
        out_specs=P("store", "mp"),
        check_vma=False,
    )
```

```python
import functools

import jax
import jax.numpy as jnp
from jax import lax
from jax.experimental import pallas as pl
from jax.experimental.pallas import tpu as pltpu
from jax.sharding import PartitionSpec as P

MESH = pl.DeviceIdType.MESH
STEPS = 4
SCALE = 0.5
EPS = 1e-05
HOPS = (2, 1, 3)
PLACE = {2: 0, 0: 1, 1: 2, 3: 3}
BF = jnp.bfloat16
F32 = jnp.float32


def kernel(
    parts, groups, tok, gain, w, down, up, plan, tgt, slt, out,
    w2, dn, un, acts, ext, sbuf, rbuf, xbuf, xrec, own, early, xown, sown, delta, scale, state, ids,
    gbuf, tbuf, sbuf_slot, i_sem, o_sem,
    w_send, w_recv, w_loc, a_send, a_recv, a_loc,
    g_send, g_recv, e_send, e_recv, r_send, r_recv, x_send, x_recv, pair,
):
    rows_all, width = tok.shape
    rows = rows_all // parts
    block = rows_all // groups
    deep = block // 2
    slots = down.shape[0]
    half = slots // 2
    features = gain.shape[1]
    s = lax.axis_index("store")
    m = lax.axis_index("mp")
    z, c = s // 2, s % 2
    y, x = m // 4, m % 4
    p = x * (1 - c) + y * c
    q = y * (1 - c) + x * c

    def mp_of(pp, qq):
        return (qq * 4 + pp) * (1 - c) + (pp * 4 + qq) * c

    def p_peer(k):
        return (s, mp_of((p + k) % 4, q))

    def q_peer(k):
        return (s, mp_of(p, (q + k) % 4))

    def z_peer(k):
        return (((z + k) % 4) * 2 + c, m)

    mate = (z * 2 + 1 - c, m)

    def remote(src, dst, send, recv, device):
        return pltpu.make_async_remote_copy(
            src_ref=src, dst_ref=dst, send_sem=send, recv_sem=recv,
            device_id=device, device_id_type=MESH,
        )

    inputs = [
        pltpu.make_async_copy(tok, state, i_sem.at[0]),
        pltpu.make_async_copy(
            gain.at[:, pl.ds(pl.multiple_of(m * width, 128), width)], gbuf, i_sem.at[1]
        ),
        pltpu.make_async_copy(tgt, tbuf, i_sem.at[2]),
        pltpu.make_async_copy(slt, sbuf_slot, i_sem.at[3]),
    ]
    for cp in inputs:
        cp.start()

    barrier = pltpu.get_barrier_semaphore()
    for k in HOPS:
        pl.semaphore_signal(barrier, inc=1, device_id=p_peer(k), device_id_type=MESH)
        pl.semaphore_signal(barrier, inc=1, device_id=q_peer(k), device_id_type=MESH)
    for k in (1, 3):
        pl.semaphore_signal(barrier, inc=1, device_id=z_peer(k), device_id_type=MESH)
    pl.semaphore_signal(barrier, inc=1, device_id=mate, device_id_type=MESH)
    pl.semaphore_wait(barrier, 9)

    lo, hi = pl.ds(0, half), pl.ds(half, half)
    s_left, s_right, s_far = ((z + 3) % 4) * 2 + c, ((z + 1) % 4) * 2 + c, ((z + 2) % 4) * 2 + c

    def adapter_copies(f, src, dst):
        def go(i, a, b, device):
            return remote(a, b, a_send.at[f, i], a_recv.at[f, i], device)

        here = [
            go(0, src.at[lo], dst.at[s, lo], z_peer(1)),
            go(1, src.at[hi], dst.at[s, hi], z_peer(1)),
            go(2, src.at[hi], dst.at[s, hi], z_peer(3)),
            go(3, src.at[lo], dst.at[s, lo], z_peer(3)),
            go(4, src, dst.at[s], mate),
        ]
        on = [
            go(5, dst.at[s_left, lo], dst.at[s_left, lo], z_peer(1)),
            go(6, dst.at[s_right, hi], dst.at[s_right, hi], z_peer(3)),
        ]
        across = [
            go(7 + i, dst.at[o, part], dst.at[o, part], mate)
            for i, (o, part) in enumerate(
                ((s_left, lo), (s_right, hi), (s_left, hi), (s_right, lo), (s_far, lo), (s_far, hi))
            )
        ]
        keep = pltpu.make_async_copy(src, dst.at[s], a_loc.at[f])
        return here, on, across, keep

    d_here, d_on, d_across, d_keep = adapter_copies(0, down, dn)
    u_here, u_on, u_across, u_keep = adapter_copies(1, up, un)

    def begin(here, keep):
        for i in (0, 2, 1, 3, 4):
            here[i].start()
        keep.start()

    begin(d_here, d_keep)

    w_out = []
    for i, k in enumerate(HOPS):
        for j in range(4):
            first = pl.multiple_of(mp_of((p + j) % 4, (q + k) % 4) * width, 128)
            w_out.append(
                remote(
                    w.at[pl.ds(first, width)],
                    w2.at[pl.ds(j * width, width), pl.ds(PLACE[4 - k] * width, width)],
                    w_send.at[i, j], w_recv.at[i, j], q_peer(k),
                )
            )
    w_keep = []
    for j in range(4):
        first = pl.multiple_of(mp_of((p + j) % 4, q) * width, 128)
        w_keep.append(
            pltpu.make_async_copy(
                w.at[pl.ds(first, width)],
                w2.at[pl.ds(j * width, width), pl.ds(PLACE[0] * width, width)],
                w_loc.at[j],
            )
        )

    low = lax.broadcasted_iota(jnp.int32, (deep, 128), 1) < 64
    diagonal = lax.broadcasted_iota(jnp.int32, (block, 128), 0) == lax.broadcasted_iota(
        jnp.int32, (block, 128), 1
    )
    line = lax.broadcasted_iota(jnp.int32, (16, 128), 0)

    def part(h):
        return pl.ds(pl.multiple_of(h * rows, rows), rows)

    def group(g):
        return pl.ds(pl.multiple_of(g * block, block), block)

    def act_copies(h, par):
        return [
            remote(
                acts.at[par, part(h), pl.ds(0, width)],
                acts.at[par, part(h), pl.ds((4 - k) * width, width)],
                g_send.at[par, h, i], g_recv.at[par, h, i], p_peer(k),
            )
            for i, k in enumerate(HOPS)
        ]

    def ext_copies(g, par):
        return [
            remote(
                ext.at[par, g, 0], ext.at[par, g, 4 - k],
                e_send.at[par, g, i], e_recv.at[par, g, i], p_peer(k),
            )
            for i, k in enumerate(HOPS)
        ]

    def sum_copies(h, par):
        return [
            remote(
                sbuf.at[par, i, part(h)], rbuf.at[par, i, part(h)],
                r_send.at[par, h, i], r_recv.at[par, h, i], q_peer(k),
            )
            for i, k in enumerate(HOPS)
        ]

    def inner_copies(g, par):
        return [
            remote(
                xbuf.at[par, g], xrec.at[par, g, i],
                x_send.at[par, g, i], x_recv.at[par, g, i], q_peer(k),
            )
            for i, k in enumerate(HOPS)
        ]


    def send_scaled(h, par):
        acts[par, part(h), 0:width] = (state[part(h)].astype(F32) * gbuf[...]).astype(BF)
        for cp in act_copies(h, par):
            cp.start()

    def as_column(row):
        return jnp.sum(jnp.where(diagonal, row, 0.0), axis=1, keepdims=True)

    def packed(inner, square):
        top = square.astype(BF).astype(F32)
        tail = jnp.where(line == 0, top, jnp.where(line == 1, square - top, 0.0))
        return inner.astype(BF), tail.astype(BF)

    def send_inner(g, par):
        now = state[group(g)].astype(F32)
        square = jnp.sum(now * now, axis=1, keepdims=True)
        square = jnp.sum(jnp.where(diagonal, square, 0.0), axis=0, keepdims=True)
        mine = acts[par, group(g), 0:width]
        who = ids[group(g)]
        acc = jnp.zeros((block, 128), F32)
        for a in range(8):
            value = lax.dot_general(
                mine, dn[a], (((1,), (1,)), ((), ())), preferred_element_type=F32
            )
            for t in range(4):
                acc += jnp.where(
                    who == float(a * 8 + 2 * t), value[:, t * 128:(t + 1) * 128], 0.0
                )
        acc += pltpu.roll(acc, 64, 1)
        body, tail = packed(jnp.where(low, acc[:deep], acc[deep:]), square)
        ext[par, g, 0, 0:deep] = body
        ext[par, g, 0, deep:deep + 16] = tail
        for cp in ext_copies(g, par):
            cp.start()

    def arrive(h, par):
        for cp in act_copies(h, par):
            cp.wait()

    def far(h, par):
        value = jnp.dot(acts[par, part(h)], w2[:, 0:2 * width], preferred_element_type=F32)
        sbuf[par, 0, part(h)] = value[:, :width].astype(BF)
        sum_copies(h, par)[0].start()
        own[part(h)] = value[:, width:]

    def send_near(h, par, value):
        copies = sum_copies(h, par)
        value = value.astype(BF)
        sbuf[par, 1, part(h)] = value[:, :width]
        copies[1].start()
        sbuf[par, 2, part(h)] = value[:, width:]
        copies[2].start()

    def multiply(h, par, first):
        @pl.when(jnp.logical_not(first))
        def _():
            arrive(h, par)
            far(h, par)
            send_near(
                h, par,
                jnp.dot(acts[par, part(h)], w2[:, 2 * width:], preferred_element_type=F32),
            )

        @pl.when(first)
        def _():
            last = jnp.dot(
                acts[par, part(h), 3 * width:], w2[3 * width:, 2 * width:],
                preferred_element_type=F32,
            )
            send_near(h, par, early[part(h)] + last)

    def forward(g, par):
        for cp in ext_copies(g, par):
            cp.wait()
        both = ext[par, g, 0].astype(F32)
        for i in range(1, 4):
            both += ext[par, g, i].astype(F32)
        inner, square = both[:deep], both[deep:deep + 1] + both[deep + 1:deep + 2]
        body, tail = packed(inner, square)
        xbuf[par, g, 0:deep] = body
        xbuf[par, g, deep:deep + 16] = tail
        for cp in inner_copies(g, par):
            cp.start()
        xown[g] = inner
        sown[g] = jnp.broadcast_to(square, (8, 128))

    def adapt(g, par):
        for cp in inner_copies(g, par):
            cp.wait()
        both = xrec[par, g, 0].astype(F32)
        for i in range(1, 3):
            both += xrec[par, g, i].astype(F32)
        square = both[deep:deep + 1] + both[deep + 1:deep + 2] + sown[g, 0:1]
        factor = as_column(lax.rsqrt(square * (1.0 / features) + EPS))
        scale[group(g)] = jnp.broadcast_to(factor, (block, 128))
        inner = both[:deep] + xown[g]
        other = pltpu.roll(inner, 64, 1)
        inner = jnp.concatenate([jnp.where(low, inner, other), jnp.where(low, other, inner)], 0)
        inner = (inner * factor).astype(BF).astype(F32)
        who = ids[group(g)]
        outer = jnp.zeros((block, width), F32)
        for a in range(8):
            spread = jnp.concatenate(
                [
                    jnp.where(who == float(a * 8 + 2 * t), inner, 0.0).astype(BF)
                    for t in range(4)
                ],
                axis=1,
            )
            outer += jnp.dot(spread, un[a], preferred_element_type=F32)
        delta[group(g)] = (SCALE * outer).astype(BF)

    def finish(h, par):
        for cp in sum_copies(h, par):
            cp.wait()
        base = own[part(h)]
        for i in range(3):
            base += rbuf[par, i, part(h)].astype(F32)
        factor = jnp.concatenate([scale[part(h)]] * (width // 128), axis=1)
        now = state[part(h)].astype(F32) + base * factor + delta[part(h)].astype(F32)
        state[part(h)] = now.astype(BF)

    def result(h):
        return pltpu.make_async_copy(state.at[part(h)], out.at[part(h)], o_sem.at[h])

    inputs[0].wait()
    inputs[1].wait()

    @pl.loop(0, parts)
    def _(h):
        send_scaled(h, 0)

    for j in range(4):
        w_out[j].start()
    for j in range(4):
        for i in (1, 2):
            w_out[i * 4 + j].start()
    for cp in w_keep:
        cp.start()

    inputs[2].wait()
    inputs[3].wait()
    wanted = tbuf[...]
    place = sbuf_slot[...]
    key = wanted * 4 + place - 8
    chosen = wanted * 8 + place
    for a in range(8):
        for r in range(4):
            hit = jnp.logical_and(place >= 8, key == a * 4 + r)
            chosen = jnp.where(hit, plan[r, a], chosen)
    chosen = chosen.astype(F32)
    upper = (lax.broadcasted_iota(jnp.int32, (block, 128), 1) >= 64).astype(F32)
    for g in range(groups):
        ids[g * block:(g + 1) * block] = as_column(chosen[:, g * block:(g + 1) * block]) - upper

    def pass_on(here, on, across):
        here[0].wait_recv()
        on[0].start()
        across[0].start()
        here[2].wait_recv()
        on[1].start()
        across[1].start()

    def pass_rest(here, across):
        here[1].wait_recv()
        across[2].start()
        here[3].wait_recv()
        across[3].start()

    def pass_last(on, across):
        on[0].wait_recv()
        across[4].start()
        on[1].wait_recv()
        across[5].start()

    def settle(here, across, keep):
        here[4].wait_recv()
        keep.wait()
        for cp in across:
            cp.wait_recv()

    def drain(here, on, across):
        for cp in here + on + across:
            cp.wait_send()

    pass_on(d_here, d_on, d_across)
    begin(u_here, u_keep)
    pass_rest(d_here, d_across)
    pass_last(d_on, d_across)
    settle(d_here, d_across, d_keep)

    @pl.loop(0, groups)
    def _(g):
        send_inner(g, 0)

    pass_on(u_here, u_on, u_across)
    pass_rest(u_here, u_across)
    for cp in w_keep + w_out[:4]:
        cp.wait()

    @pl.loop(0, parts)
    def _(h):
        arrive(h, 0)
        far(h, 0)

    @pl.loop(0, groups)
    def _(g):
        forward(g, 0)

    pass_last(u_on, u_across)
    for j in range(3):
        w_out[4 + j].wait()
        w_out[8 + j].wait()

    @pl.loop(0, parts)
    def _(h):
        early[part(h)] = jnp.dot(
            acts[0, part(h), 0:3 * width], w2[0:3 * width, 2 * width:],
            preferred_element_type=F32,
        )

    w_out[7].wait()
    w_out[11].wait()

    per = parts // groups

    @pl.loop(0, STEPS)
    def _(t):
        par = t % 2
        pl.semaphore_signal(pair, inc=1, device_id=mate, device_id_type=MESH)
        pl.semaphore_wait(pair, 1)

        @pl.loop(0, groups)
        def _(g):
            multiply(g * per, par, t == 0)

            @pl.when(t > 0)
            def _():
                forward(g, par)

            for i in range(1, per):
                multiply(g * per + i, par, t == 0)

        @pl.when(t == 0)
        def _():
            settle(u_here, u_across, u_keep)

        @pl.loop(0, groups)
        def _(g):
            adapt(g, par)

            @pl.loop(0, per)
            def _(i):
                h = g * per + i
                finish(h, par)

                @pl.when(t < STEPS - 1)
                def _():
                    send_scaled(h, 1 - par)

                @pl.when(t == STEPS - 1)
                def _():
                    result(h).start()

            @pl.when(t < STEPS - 1)
            def _():
                send_inner(g, 1 - par)

    drain(d_here, d_on, d_across)
    drain(u_here, u_on, u_across)
    for h in range(parts):
        result(h).wait()


PARTS = 4
GROUPS = 2


def local(tokens, gain, base_weight, down, up, plan, target, slot):
    rows_all, width = tokens.shape
    owned, rank, _ = down.shape
    stores = 8
    lines = rows_all // GROUPS // 2 + 16
    dma = pltpu.SemaphoreType.DMA
    anywhere = pl.BlockSpec(memory_space=pl.ANY)
    return pl.pallas_call(
        functools.partial(kernel, PARTS, GROUPS),
        out_shape=jax.ShapeDtypeStruct((rows_all, width), BF),
        in_specs=[
            anywhere, anywhere, anywhere, anywhere, anywhere,
            pl.BlockSpec(memory_space=pltpu.SMEM), anywhere, anywhere,
        ],
        out_specs=anywhere,
        scratch_shapes=[
            pltpu.VMEM((4 * width, 4 * width), BF),
            pltpu.VMEM((stores, owned * rank, width), BF),
            pltpu.VMEM((stores, owned * rank, width), BF),
            pltpu.VMEM((2, rows_all, 4 * width), BF),
            pltpu.VMEM((2, GROUPS, 4, lines, 128), BF),
            pltpu.VMEM((2, 3, rows_all, width), BF),
            pltpu.VMEM((2, 3, rows_all, width), BF),
            pltpu.VMEM((2, GROUPS, lines, 128), BF),
            pltpu.VMEM((2, GROUPS, 3, lines, 128), BF),
            pltpu.VMEM((rows_all, width), F32),
            pltpu.VMEM((rows_all, 2 * width), F32),
            pltpu.VMEM((GROUPS, lines - 16, 128), F32),
            pltpu.VMEM((GROUPS, 8, 128), F32),
            pltpu.VMEM((rows_all, width), BF),
            pltpu.VMEM((rows_all, 128), F32),
            pltpu.VMEM((rows_all, width), BF),
            pltpu.VMEM((rows_all, 128), F32),
            pltpu.VMEM((1, width), F32),
            pltpu.VMEM((1, rows_all), jnp.int32),
            pltpu.VMEM((1, rows_all), jnp.int32),
            dma((4,)), dma((PARTS,)),
            dma((3, 4)), dma((3, 4)), dma((4,)),
            dma((2, 13)), dma((2, 13)), dma((2,)),
            dma((2, PARTS, 3)), dma((2, PARTS, 3)),
            dma((2, GROUPS, 3)), dma((2, GROUPS, 3)),
            dma((2, PARTS, 3)), dma((2, PARTS, 3)),
            dma((2, GROUPS, 3)), dma((2, GROUPS, 3)),
            pltpu.SemaphoreType.REGULAR,
        ],
        compiler_params=pltpu.CompilerParams(
            collective_id=0, has_side_effects=True, vmem_limit_bytes=56 << 20
        ),
    )(
        tokens, gain.reshape(1, -1), base_weight,
        down.reshape(owned * rank, width), up.reshape(owned * rank, width),
        plan.T, target.reshape(1, -1), slot.reshape(1, -1),
    )


def solution(mesh):
    return jax.shard_map(
        local,
        mesh=mesh,
        in_specs=(
            P("store", "mp"),
            P(),
            P(None, "mp"),
            P("store", None, "mp"),
            P("store", None, "mp"),
            P(),
            P("store", None),
            P("store"),
        ),
        out_specs=P("store", "mp"),
        check_vma=False,
    )
```

```python
import functools

import jax
import jax.numpy as jnp
from jax import lax
from jax.experimental import pallas as pl
from jax.experimental.pallas import tpu as pltpu
from jax.sharding import PartitionSpec as P

MESH = pl.DeviceIdType.MESH
STEPS = 4
SCALE = 0.5
EPS = 1e-05
HOPS = (2, 1, 3)
PLACE = {2: 0, 0: 1, 1: 2, 3: 3}
BF = jnp.bfloat16
F32 = jnp.float32


def kernel(
    parts, groups, tok, gain, w, down, up, plan, tgt, slt, out,
    w2, dn, un, acts, ext, sbuf, rbuf, xbuf, xrec, own, early, xown, sown, delta, scale, state, ids,
    gbuf, tbuf, sbuf_slot, pbuf, i_sem, o_sem,
    w_send, w_recv, w_loc, a_send, a_recv, a_loc,
    g_send, g_recv, e_send, e_recv, r_send, r_recv, x_send, x_recv, pair,
):
    rows_all, width = tok.shape
    rows = rows_all // parts
    block = rows_all // groups
    deep = block // 2
    slots = down.shape[0]
    half = slots // 2
    features = gain.shape[1]
    s = lax.axis_index("store")
    m = lax.axis_index("mp")
    z, c = s // 2, s % 2
    y, x = m // 4, m % 4
    p = x * (1 - c) + y * c
    q = y * (1 - c) + x * c

    def mp_of(pp, qq):
        return (qq * 4 + pp) * (1 - c) + (pp * 4 + qq) * c

    def p_peer(k):
        return (s, mp_of((p + k) % 4, q))

    def q_peer(k):
        return (s, mp_of(p, (q + k) % 4))

    def z_peer(k):
        return (((z + k) % 4) * 2 + c, m)

    mate = (z * 2 + 1 - c, m)

    def remote(src, dst, send, recv, device):
        return pltpu.make_async_remote_copy(
            src_ref=src, dst_ref=dst, send_sem=send, recv_sem=recv,
            device_id=device, device_id_type=MESH,
        )

    inputs = [
        pltpu.make_async_copy(tok, state, i_sem.at[0]),
        pltpu.make_async_copy(
            gain.at[:, pl.ds(pl.multiple_of(m * width, 128), width)], gbuf, i_sem.at[1]
        ),
        pltpu.make_async_copy(tgt, tbuf, i_sem.at[2]),
        pltpu.make_async_copy(slt, sbuf_slot, i_sem.at[3]),
        pltpu.make_async_copy(plan, pbuf, i_sem.at[4]),
    ]
    for cp in inputs:
        cp.start()

    barrier = pltpu.get_barrier_semaphore()
    for k in HOPS:
        pl.semaphore_signal(barrier, inc=1, device_id=p_peer(k), device_id_type=MESH)
        pl.semaphore_signal(barrier, inc=1, device_id=q_peer(k), device_id_type=MESH)
    for k in (1, 3):
        pl.semaphore_signal(barrier, inc=1, device_id=z_peer(k), device_id_type=MESH)
    pl.semaphore_signal(barrier, inc=1, device_id=mate, device_id_type=MESH)
    pl.semaphore_wait(barrier, 9)

    lo, hi = pl.ds(0, half), pl.ds(half, half)
    s_left, s_right, s_far = ((z + 3) % 4) * 2 + c, ((z + 1) % 4) * 2 + c, ((z + 2) % 4) * 2 + c

    def adapter_copies(f, src, dst):
        def go(i, a, b, device):
            return remote(a, b, a_send.at[f, i], a_recv.at[f, i], device)

        here = [
            go(0, src.at[lo], dst.at[s, lo], z_peer(1)),
            go(1, src.at[hi], dst.at[s, hi], z_peer(1)),
            go(2, src.at[hi], dst.at[s, hi], z_peer(3)),
            go(3, src.at[lo], dst.at[s, lo], z_peer(3)),
            go(4, src, dst.at[s], mate),
        ]
        on = [
            go(5, dst.at[s_left, lo], dst.at[s_left, lo], z_peer(1)),
            go(6, dst.at[s_right, hi], dst.at[s_right, hi], z_peer(3)),
        ]
        across = [
            go(7 + i, dst.at[o, part], dst.at[o, part], mate)
            for i, (o, part) in enumerate(
                ((s_left, lo), (s_right, hi), (s_left, hi), (s_right, lo), (s_far, lo), (s_far, hi))
            )
        ]
        keep = pltpu.make_async_copy(src, dst.at[s], a_loc.at[f])
        return here, on, across, keep

    d_here, d_on, d_across, d_keep = adapter_copies(0, down, dn)
    u_here, u_on, u_across, u_keep = adapter_copies(1, up, un)

    def begin(here, keep):
        for i in (0, 2, 1, 3, 4):
            here[i].start()
        keep.start()

    begin(d_here, d_keep)

    w_out = []
    for i, k in enumerate(HOPS):
        for j in range(4):
            first = pl.multiple_of(mp_of((p + j) % 4, (q + k) % 4) * width, 128)
            w_out.append(
                remote(
                    w.at[pl.ds(first, width)],
                    w2.at[pl.ds(j * width, width), pl.ds(PLACE[4 - k] * width, width)],
                    w_send.at[i, j], w_recv.at[i, j], q_peer(k),
                )
            )
    w_keep = []
    for j in range(4):
        first = pl.multiple_of(mp_of((p + j) % 4, q) * width, 128)
        w_keep.append(
            pltpu.make_async_copy(
                w.at[pl.ds(first, width)],
                w2.at[pl.ds(j * width, width), pl.ds(PLACE[0] * width, width)],
                w_loc.at[j],
            )
        )

    low = lax.broadcasted_iota(jnp.int32, (deep, 128), 1) < 64
    diagonal = lax.broadcasted_iota(jnp.int32, (block, 128), 0) == lax.broadcasted_iota(
        jnp.int32, (block, 128), 1
    )
    line = lax.broadcasted_iota(jnp.int32, (16, 128), 0)

    def part(h):
        return pl.ds(pl.multiple_of(h * rows, rows), rows)

    def group(g):
        return pl.ds(pl.multiple_of(g * block, block), block)

    def act_copies(h, par):
        return [
            remote(
                acts.at[par, part(h), pl.ds(0, width)],
                acts.at[par, part(h), pl.ds((4 - k) * width, width)],
                g_send.at[par, h, i], g_recv.at[par, h, i], p_peer(k),
            )
            for i, k in enumerate(HOPS)
        ]

    def ext_copies(g, par, peer=q_peer):
        return [
            remote(
                ext.at[par, g, 0], ext.at[par, g, 4 - k],
                e_send.at[par, g, i], e_recv.at[par, g, i], peer(k),
            )
            for i, k in enumerate(HOPS)
        ]

    def sum_copies(h, par):
        return [
            remote(
                sbuf.at[par, i, part(h)], rbuf.at[par, i, part(h)],
                r_send.at[par, h, i], r_recv.at[par, h, i], q_peer(k),
            )
            for i, k in enumerate(HOPS)
        ]

    def inner_copies(g, par, peer=p_peer):
        return [
            remote(
                xbuf.at[par, g], xrec.at[par, g, i],
                x_send.at[par, g, i], x_recv.at[par, g, i], peer(k),
            )
            for i, k in enumerate(HOPS)
        ]


    def send_scaled(h, par):
        acts[par, part(h), 0:width] = (state[part(h)].astype(F32) * gbuf[...]).astype(BF)
        for cp in act_copies(h, par):
            cp.start()

    def as_column(row):
        return jnp.sum(jnp.where(diagonal, row, 0.0), axis=1, keepdims=True)

    def packed(inner, square):
        top = square.astype(BF).astype(F32)
        tail = jnp.where(line == 0, top, jnp.where(line == 1, square - top, 0.0))
        return inner.astype(BF), tail.astype(BF)

    def send_inner(g, par, peer=q_peer):
        now = state[group(g)].astype(F32)
        square = jnp.sum(now * now, axis=1, keepdims=True)
        square = jnp.sum(jnp.where(diagonal, square, 0.0), axis=0, keepdims=True)
        mine = acts[par, group(g), 0:width]
        who = ids[group(g)]
        acc = jnp.zeros((block, 128), F32)
        for a in range(8):
            value = lax.dot_general(
                mine, dn[a], (((1,), (1,)), ((), ())), preferred_element_type=F32
            )
            for t in range(4):
                acc += jnp.where(
                    who == float(a * 8 + 2 * t), value[:, t * 128:(t + 1) * 128], 0.0
                )
        acc += pltpu.roll(acc, 64, 1)
        body, tail = packed(jnp.where(low, acc[:deep], acc[deep:]), square)
        ext[par, g, 0, 0:deep] = body
        ext[par, g, 0, deep:deep + 16] = tail
        for cp in ext_copies(g, par, peer):
            cp.start()

    def arrive(h, par):
        for cp in act_copies(h, par):
            cp.wait()

    def far(h, par):
        value = jnp.dot(acts[par, part(h)], w2[:, 0:2 * width], preferred_element_type=F32)
        sbuf[par, 0, part(h)] = value[:, :width].astype(BF)
        sum_copies(h, par)[0].start()
        own[part(h)] = value[:, width:]

    def send_near(h, par, value):
        copies = sum_copies(h, par)
        value = value.astype(BF)
        sbuf[par, 1, part(h)] = value[:, :width]
        copies[1].start()
        sbuf[par, 2, part(h)] = value[:, width:]
        copies[2].start()

    def multiply(h, par, first):
        @pl.when(jnp.logical_not(first))
        def _():
            arrive(h, par)
            far(h, par)
            send_near(
                h, par,
                jnp.dot(acts[par, part(h)], w2[:, 2 * width:], preferred_element_type=F32),
            )

        @pl.when(first)
        def _():
            last = jnp.dot(
                acts[par, part(h), 3 * width:], w2[3 * width:, 2 * width:],
                preferred_element_type=F32,
            )
            send_near(h, par, early[part(h)] + last)

    def forward(g, par, peer=p_peer):
        for cp in ext_copies(g, par):
            cp.wait()
        both = ext[par, g, 0].astype(F32)
        for i in range(1, 4):
            both += ext[par, g, i].astype(F32)
        inner, square = both[:deep], both[deep:deep + 1] + both[deep + 1:deep + 2]
        body, tail = packed(inner, square)
        xbuf[par, g, 0:deep] = body
        xbuf[par, g, deep:deep + 16] = tail
        for cp in inner_copies(g, par, peer):
            cp.start()
        xown[g] = inner
        sown[g] = jnp.broadcast_to(square, (8, 128))

    def adapt(g, par):
        for cp in inner_copies(g, par):
            cp.wait()
        both = xrec[par, g, 0].astype(F32)
        for i in range(1, 3):
            both += xrec[par, g, i].astype(F32)
        square = both[deep:deep + 1] + both[deep + 1:deep + 2] + sown[g, 0:1]
        factor = as_column(lax.rsqrt(square * (1.0 / features) + EPS))
        scale[group(g)] = jnp.broadcast_to(factor, (block, 128))
        inner = both[:deep] + xown[g]
        other = pltpu.roll(inner, 64, 1)
        inner = jnp.concatenate([jnp.where(low, inner, other), jnp.where(low, other, inner)], 0)
        inner = (inner * factor).astype(BF).astype(F32)
        who = ids[group(g)]
        outer = jnp.zeros((block, width), F32)
        for a in range(8):
            spread = jnp.concatenate(
                [
                    jnp.where(who == float(a * 8 + 2 * t), inner, 0.0).astype(BF)
                    for t in range(4)
                ],
                axis=1,
            )
            outer += jnp.dot(spread, un[a], preferred_element_type=F32)
        delta[group(g)] = (SCALE * outer).astype(BF)

    def finish(h, par):
        for cp in sum_copies(h, par):
            cp.wait()
        base = own[part(h)]
        for i in range(3):
            base += rbuf[par, i, part(h)].astype(F32)
        factor = jnp.concatenate([scale[part(h)]] * (width // 128), axis=1)
        now = state[part(h)].astype(F32) + base * factor + delta[part(h)].astype(F32)
        state[part(h)] = now.astype(BF)

    def result(h):
        return pltpu.make_async_copy(state.at[part(h)], out.at[part(h)], o_sem.at[h])

    for j in range(4):
        w_out[j].start()
    for j in range(4):
        for i in (1, 2):
            w_out[i * 4 + j].start()
    for cp in w_keep:
        cp.start()

    inputs[0].wait()
    inputs[1].wait()

    @pl.loop(0, parts)
    def _(h):
        send_scaled(h, 0)

    inputs[2].wait()
    inputs[3].wait()
    inputs[4].wait()
    wanted = tbuf[...]
    place = sbuf_slot[...]
    key = wanted * 4 + place - 8
    chosen = wanted * 8 + place
    for a in range(8):
        for r in range(4):
            hit = jnp.logical_and(place >= 8, key == a * 4 + r)
            chosen = jnp.where(hit, pbuf[r, a], chosen)
    chosen = chosen.astype(F32)
    upper = (lax.broadcasted_iota(jnp.int32, (block, 128), 1) >= 64).astype(F32)
    for g in range(groups):
        ids[g * block:(g + 1) * block] = as_column(chosen[:, g * block:(g + 1) * block]) - upper

    def pass_on(here, on, across):
        here[0].wait_recv()
        on[0].start()
        across[0].start()
        here[2].wait_recv()
        on[1].start()
        across[1].start()

    def pass_rest(here, across):
        here[1].wait_recv()
        across[2].start()
        here[3].wait_recv()
        across[3].start()

    def pass_last(on, across):
        on[0].wait_recv()
        across[4].start()
        on[1].wait_recv()
        across[5].start()

    def settle(here, across, keep):
        here[4].wait_recv()
        keep.wait()
        for cp in across:
            cp.wait_recv()

    def drain(here, on, across):
        for cp in here + on + across:
            cp.wait_send()

    pass_on(d_here, d_on, d_across)
    begin(u_here, u_keep)
    pass_rest(d_here, d_across)
    pass_last(d_on, d_across)
    settle(d_here, d_across, d_keep)

    @pl.loop(0, groups)
    def _(g):
        send_inner(g, 0, p_peer)

    pass_on(u_here, u_on, u_across)
    pass_rest(u_here, u_across)
    for cp in w_keep + w_out[:4]:
        cp.wait()

    @pl.loop(0, parts)
    def _(h):
        arrive(h, 0)
        far(h, 0)

    @pl.loop(0, groups)
    def _(g):
        forward(g, 0, q_peer)

    pass_last(u_on, u_across)
    for j in range(3):
        w_out[4 + j].wait()
        w_out[8 + j].wait()

    @pl.loop(0, parts)
    def _(h):
        early[part(h)] = jnp.dot(
            acts[0, part(h), 0:3 * width], w2[0:3 * width, 2 * width:],
            preferred_element_type=F32,
        )

    w_out[7].wait()
    w_out[11].wait()

    per = parts // groups

    @pl.loop(0, STEPS)
    def _(t):
        par = t % 2
        pl.semaphore_signal(pair, inc=1, device_id=mate, device_id_type=MESH)
        pl.semaphore_wait(pair, 1)

        @pl.loop(0, groups)
        def _(g):
            multiply(g * per, par, t == 0)

            @pl.when(t > 0)
            def _():
                forward(g, par)

            for i in range(1, per):
                multiply(g * per + i, par, t == 0)

        @pl.when(t == 0)
        def _():
            settle(u_here, u_across, u_keep)
            drain(d_here, d_on, d_across)
            drain(u_here, u_on, u_across)

        @pl.loop(0, groups)
        def _(g):
            adapt(g, par)

            @pl.loop(0, per)
            def _(i):
                h = g * per + i
                finish(h, par)

                @pl.when(t < STEPS - 1)
                def _():
                    send_scaled(h, 1 - par)

                @pl.when(t == STEPS - 1)
                def _():
                    result(h).start()

            @pl.when(t < STEPS - 1)
            def _():
                send_inner(g, 1 - par)

    for h in range(parts):
        result(h).wait()


PARTS = 4
GROUPS = 2


def local(tokens, gain, base_weight, down, up, plan, target, slot):
    rows_all, width = tokens.shape
    owned, rank, _ = down.shape
    stores = 8
    lines = rows_all // GROUPS // 2 + 16
    dma = pltpu.SemaphoreType.DMA
    anywhere = pl.BlockSpec(memory_space=pl.ANY)
    return pl.pallas_call(
        functools.partial(kernel, PARTS, GROUPS),
        out_shape=jax.ShapeDtypeStruct((rows_all, width), BF),
        in_specs=[
            anywhere, anywhere, anywhere, anywhere, anywhere,
            anywhere, anywhere, anywhere,
        ],
        out_specs=anywhere,
        scratch_shapes=[
            pltpu.VMEM((4 * width, 4 * width), BF),
            pltpu.VMEM((stores, owned * rank, width), BF),
            pltpu.VMEM((stores, owned * rank, width), BF),
            pltpu.VMEM((2, rows_all, 4 * width), BF),
            pltpu.VMEM((2, GROUPS, 4, lines, 128), BF),
            pltpu.VMEM((2, 3, rows_all, width), BF),
            pltpu.VMEM((2, 3, rows_all, width), BF),
            pltpu.VMEM((2, GROUPS, lines, 128), BF),
            pltpu.VMEM((2, GROUPS, 3, lines, 128), BF),
            pltpu.VMEM((rows_all, width), F32),
            pltpu.VMEM((rows_all, 2 * width), F32),
            pltpu.VMEM((GROUPS, lines - 16, 128), F32),
            pltpu.VMEM((GROUPS, 8, 128), F32),
            pltpu.VMEM((rows_all, width), BF),
            pltpu.VMEM((rows_all, 128), F32),
            pltpu.VMEM((rows_all, width), BF),
            pltpu.VMEM((rows_all, 128), F32),
            pltpu.VMEM((1, width), F32),
            pltpu.VMEM((1, rows_all), jnp.int32),
            pltpu.VMEM((1, rows_all), jnp.int32),
            pltpu.SMEM((4, 8), jnp.int32),
            dma((5,)), dma((PARTS,)),
            dma((3, 4)), dma((3, 4)), dma((4,)),
            dma((2, 13)), dma((2, 13)), dma((2,)),
            dma((2, PARTS, 3)), dma((2, PARTS, 3)),
            dma((2, GROUPS, 3)), dma((2, GROUPS, 3)),
            dma((2, PARTS, 3)), dma((2, PARTS, 3)),
            dma((2, GROUPS, 3)), dma((2, GROUPS, 3)),
            pltpu.SemaphoreType.REGULAR,
        ],
        compiler_params=pltpu.CompilerParams(
            collective_id=0, has_side_effects=True, vmem_limit_bytes=56 << 20
        ),
    )(
        tokens, gain.reshape(1, -1), base_weight,
        down.reshape(owned * rank, width), up.reshape(owned * rank, width),
        plan.T, target.reshape(1, -1), slot.reshape(1, -1),
    )


def solution(mesh):
    return jax.shard_map(
        local,
        mesh=mesh,
        in_specs=(
            P("store", "mp"),
            P(),
            P(None, "mp"),
            P("store", None, "mp"),
            P("store", None, "mp"),
            P(),
            P("store", None),
            P("store"),
        ),
        out_specs=P("store", "mp"),
        check_vma=False,
    )
```

```python
import functools

import jax
import jax.numpy as jnp
from jax import lax
from jax.experimental import pallas as pl
from jax.experimental.pallas import tpu as pltpu
from jax.sharding import PartitionSpec as P

MESH = pl.DeviceIdType.MESH
STEPS = 4
SCALE = 0.5
EPS = 1e-05
HOPS = (2, 1, 3)
PLACE = {2: 0, 0: 1, 1: 2, 3: 3}
BF = jnp.bfloat16
F32 = jnp.float32


def kernel(
    parts, groups, tok, gain, w, down, up, plan, tgt, slt, out,
    w2, dn, un, acts, ext, sbuf, rbuf, xbuf, xrec, own, early, xown, sown, delta, scale, state, ids,
    gbuf, tbuf, sbuf_slot, pbuf, i_sem, o_sem,
    w_send, w_recv, w_loc, a_send, a_recv, a_loc,
    g_send, g_recv, e_send, e_recv, r_send, r_recv, x_send, x_recv, pair,
):
    rows_all, width = tok.shape
    rows = rows_all // parts
    block = rows_all // groups
    deep = block // 2
    slots = down.shape[0]
    half = slots // 2
    features = gain.shape[1]
    s = lax.axis_index("store")
    m = lax.axis_index("mp")
    z, c = s // 2, s % 2
    y, x = m // 4, m % 4
    p = x * (1 - c) + y * c
    q = y * (1 - c) + x * c

    def mp_of(pp, qq):
        return (qq * 4 + pp) * (1 - c) + (pp * 4 + qq) * c

    def p_peer(k):
        return (s, mp_of((p + k) % 4, q))

    def q_peer(k):
        return (s, mp_of(p, (q + k) % 4))

    def z_peer(k):
        return (((z + k) % 4) * 2 + c, m)

    mate = (z * 2 + 1 - c, m)

    def remote(src, dst, send, recv, device):
        return pltpu.make_async_remote_copy(
            src_ref=src, dst_ref=dst, send_sem=send, recv_sem=recv,
            device_id=device, device_id_type=MESH,
        )

    inputs = [
        pltpu.make_async_copy(tok, state, i_sem.at[0]),
        pltpu.make_async_copy(
            gain.at[:, pl.ds(pl.multiple_of(m * width, 128), width)], gbuf, i_sem.at[1]
        ),
        pltpu.make_async_copy(tgt, tbuf, i_sem.at[2]),
        pltpu.make_async_copy(slt, sbuf_slot, i_sem.at[3]),
        pltpu.make_async_copy(plan, pbuf, i_sem.at[4]),
    ]
    for cp in inputs:
        cp.start()

    barrier = pltpu.get_barrier_semaphore()
    for k in HOPS:
        pl.semaphore_signal(barrier, inc=1, device_id=p_peer(k), device_id_type=MESH)
        pl.semaphore_signal(barrier, inc=1, device_id=q_peer(k), device_id_type=MESH)
    for k in (1, 3):
        pl.semaphore_signal(barrier, inc=1, device_id=z_peer(k), device_id_type=MESH)
    pl.semaphore_signal(barrier, inc=1, device_id=mate, device_id_type=MESH)
    pl.semaphore_wait(barrier, 9)

    lo, hi = pl.ds(0, half), pl.ds(half, half)
    s_left, s_right, s_far = ((z + 3) % 4) * 2 + c, ((z + 1) % 4) * 2 + c, ((z + 2) % 4) * 2 + c

    def adapter_copies(f, src, dst):
        def go(i, a, b, device):
            return remote(a, b, a_send.at[f, i], a_recv.at[f, i], device)

        here = [
            go(0, src.at[lo], dst.at[s, lo], z_peer(1)),
            go(1, src.at[hi], dst.at[s, hi], z_peer(1)),
            go(2, src.at[hi], dst.at[s, hi], z_peer(3)),
            go(3, src.at[lo], dst.at[s, lo], z_peer(3)),
            go(4, src, dst.at[s], mate),
        ]
        on = [
            go(5, dst.at[s_left, lo], dst.at[s_left, lo], z_peer(1)),
            go(6, dst.at[s_right, hi], dst.at[s_right, hi], z_peer(3)),
        ]
        across = [
            go(7 + i, dst.at[o, part], dst.at[o, part], mate)
            for i, (o, part) in enumerate(
                ((s_left, lo), (s_right, hi), (s_left, hi), (s_right, lo), (s_far, lo), (s_far, hi))
            )
        ]
        keep = pltpu.make_async_copy(src, dst.at[s], a_loc.at[f])
        return here, on, across, keep

    d_here, d_on, d_across, d_keep = adapter_copies(0, down, dn)
    u_here, u_on, u_across, u_keep = adapter_copies(1, up, un)

    def begin(here, keep):
        for i in (0, 2, 1, 3, 4):
            here[i].start()
        keep.start()

    begin(d_here, d_keep)

    w_out = []
    for i, k in enumerate(HOPS):
        for j in range(4):
            first = pl.multiple_of(mp_of((p + j) % 4, (q + k) % 4) * width, 128)
            w_out.append(
                remote(
                    w.at[pl.ds(first, width)],
                    w2.at[pl.ds(j * width, width), pl.ds(PLACE[4 - k] * width, width)],
                    w_send.at[i, j], w_recv.at[i, j], q_peer(k),
                )
            )
    w_keep = []
    for j in range(4):
        first = pl.multiple_of(mp_of((p + j) % 4, q) * width, 128)
        w_keep.append(
            pltpu.make_async_copy(
                w.at[pl.ds(first, width)],
                w2.at[pl.ds(j * width, width), pl.ds(PLACE[0] * width, width)],
                w_loc.at[j],
            )
        )

    low = lax.broadcasted_iota(jnp.int32, (deep, 128), 1) < 64
    diagonal = lax.broadcasted_iota(jnp.int32, (block, 128), 0) == lax.broadcasted_iota(
        jnp.int32, (block, 128), 1
    )
    line = lax.broadcasted_iota(jnp.int32, (16, 128), 0)

    def part(h):
        return pl.ds(pl.multiple_of(h * rows, rows), rows)

    def group(g):
        return pl.ds(pl.multiple_of(g * block, block), block)

    def act_copies(h, par):
        return [
            remote(
                acts.at[par, part(h), pl.ds(0, width)],
                acts.at[par, part(h), pl.ds((4 - k) * width, width)],
                g_send.at[par, h, i], g_recv.at[par, h, i], p_peer(k),
            )
            for i, k in enumerate(HOPS)
        ]

    def ext_copies(g, par, peer=q_peer):
        return [
            remote(
                ext.at[par, g, 0], ext.at[par, g, 4 - k],
                e_send.at[par, g, i], e_recv.at[par, g, i], peer(k),
            )
            for i, k in enumerate(HOPS)
        ]

    def sum_copies(h, par):
        return [
            remote(
                sbuf.at[par, i, part(h)], rbuf.at[par, i, part(h)],
                r_send.at[par, h, i], r_recv.at[par, h, i], q_peer(k),
            )
            for i, k in enumerate(HOPS)
        ]

    def inner_copies(g, par, peer=p_peer):
        return [
            remote(
                xbuf.at[par, g], xrec.at[par, g, i],
                x_send.at[par, g, i], x_recv.at[par, g, i], peer(k),
            )
            for i, k in enumerate(HOPS)
        ]


    def send_scaled(h, par):
        acts[par, part(h), 0:width] = (state[part(h)].astype(F32) * gbuf[...]).astype(BF)
        for cp in act_copies(h, par):
            cp.start()

    def as_column(row):
        return jnp.sum(jnp.where(diagonal, row, 0.0), axis=1, keepdims=True)

    def packed(inner, square):
        top = square.astype(BF).astype(F32)
        tail = jnp.where(line == 0, top, jnp.where(line == 1, square - top, 0.0))
        return inner.astype(BF), tail.astype(BF)

    def send_inner(g, par, peer=q_peer):
        now = state[group(g)].astype(F32)
        square = jnp.sum(now * now, axis=1, keepdims=True)
        square = jnp.sum(jnp.where(diagonal, square, 0.0), axis=0, keepdims=True)
        mine = acts[par, group(g), 0:width]
        who = ids[group(g)]
        acc = jnp.zeros((block, 128), F32)
        for a in range(8):
            value = lax.dot_general(
                mine, dn[a], (((1,), (1,)), ((), ())), preferred_element_type=F32
            )
            for t in range(4):
                acc += jnp.where(
                    who == float(a * 8 + 2 * t), value[:, t * 128:(t + 1) * 128], 0.0
                )
        acc += pltpu.roll(acc, 64, 1)
        body, tail = packed(jnp.where(low, acc[:deep], acc[deep:]), square)
        ext[par, g, 0, 0:deep] = body
        ext[par, g, 0, deep:deep + 16] = tail
        for cp in ext_copies(g, par, peer):
            cp.start()

    def arrive(h, par):
        for cp in act_copies(h, par):
            cp.wait()

    def far(h, par):
        value = jnp.dot(acts[par, part(h)], w2[:, 0:2 * width], preferred_element_type=F32)
        sbuf[par, 0, part(h)] = value[:, :width].astype(BF)
        sum_copies(h, par)[0].start()
        own[part(h)] = value[:, width:]

    def send_near(h, par, value):
        copies = sum_copies(h, par)
        value = value.astype(BF)
        sbuf[par, 1, part(h)] = value[:, :width]
        copies[1].start()
        sbuf[par, 2, part(h)] = value[:, width:]
        copies[2].start()

    def multiply(h, par, first):
        @pl.when(jnp.logical_not(first))
        def _():
            arrive(h, par)
            far(h, par)
            send_near(
                h, par,
                jnp.dot(acts[par, part(h)], w2[:, 2 * width:], preferred_element_type=F32),
            )

        @pl.when(first)
        def _():
            last = jnp.dot(
                acts[par, part(h), 3 * width:], w2[3 * width:, 2 * width:],
                preferred_element_type=F32,
            )
            send_near(h, par, early[part(h)] + last)

    def forward(g, par, peer=p_peer):
        for cp in ext_copies(g, par):
            cp.wait()
        both = ext[par, g, 0].astype(F32)
        for i in range(1, 4):
            both += ext[par, g, i].astype(F32)
        inner, square = both[:deep], both[deep:deep + 1] + both[deep + 1:deep + 2]
        body, tail = packed(inner, square)
        xbuf[par, g, 0:deep] = body
        xbuf[par, g, deep:deep + 16] = tail
        for cp in inner_copies(g, par, peer):
            cp.start()
        xown[g] = inner
        sown[g] = jnp.broadcast_to(square, (8, 128))

    def adapt(g, par):
        for cp in inner_copies(g, par):
            cp.wait()
        both = xrec[par, g, 0].astype(F32)
        for i in range(1, 3):
            both += xrec[par, g, i].astype(F32)
        square = both[deep:deep + 1] + both[deep + 1:deep + 2] + sown[g, 0:1]
        factor = as_column(lax.rsqrt(square * (1.0 / features) + EPS))
        scale[group(g)] = jnp.broadcast_to(factor, (block, 128))
        inner = both[:deep] + xown[g]
        other = pltpu.roll(inner, 64, 1)
        inner = jnp.concatenate([jnp.where(low, inner, other), jnp.where(low, other, inner)], 0)
        inner = (inner * factor).astype(BF).astype(F32)
        who = ids[group(g)]
        outer = jnp.zeros((block, width), F32)
        for a in range(8):
            spread = jnp.concatenate(
                [
                    jnp.where(who == float(a * 8 + 2 * t), inner, 0.0).astype(BF)
                    for t in range(4)
                ],
                axis=1,
            )
            outer += jnp.dot(spread, un[a], preferred_element_type=F32)
        delta[group(g)] = (SCALE * outer).astype(BF)

    def finish(h, par):
        for cp in sum_copies(h, par):
            cp.wait()
        base = own[part(h)]
        for i in range(3):
            base += rbuf[par, i, part(h)].astype(F32)
        factor = jnp.concatenate([scale[part(h)]] * (width // 128), axis=1)
        now = state[part(h)].astype(F32) + base * factor + delta[part(h)].astype(F32)
        state[part(h)] = now.astype(BF)

    def result(h):
        return pltpu.make_async_copy(state.at[part(h)], out.at[part(h)], o_sem.at[h])

    for j in range(4):
        w_out[j].start()
    for cp in w_keep:
        cp.start()

    inputs[0].wait()
    inputs[1].wait()

    @pl.loop(0, parts)
    def _(h):
        send_scaled(h, 0)

    for j in range(4):
        for i in (1, 2):
            w_out[i * 4 + j].start()

    inputs[2].wait()
    inputs[3].wait()
    inputs[4].wait()
    wanted = tbuf[...]
    place = sbuf_slot[...]
    key = wanted * 4 + place - 8
    chosen = wanted * 8 + place
    for a in range(8):
        for r in range(4):
            hit = jnp.logical_and(place >= 8, key == a * 4 + r)
            chosen = jnp.where(hit, pbuf[r, a], chosen)
    chosen = chosen.astype(F32)
    upper = (lax.broadcasted_iota(jnp.int32, (block, 128), 1) >= 64).astype(F32)
    for g in range(groups):
        ids[g * block:(g + 1) * block] = as_column(chosen[:, g * block:(g + 1) * block]) - upper

    def pass_on(here, on, across):
        here[0].wait_recv()
        on[0].start()
        across[0].start()
        here[2].wait_recv()
        on[1].start()
        across[1].start()

    def pass_rest(here, across):
        here[1].wait_recv()
        across[2].start()
        here[3].wait_recv()
        across[3].start()

    def pass_last(on, across):
        on[0].wait_recv()
        across[4].start()
        on[1].wait_recv()
        across[5].start()

    def settle(here, across, keep):
        here[4].wait_recv()
        keep.wait()
        for cp in across:
            cp.wait_recv()

    def drain(here, on, across):
        for cp in here + on + across:
            cp.wait_send()

    pass_on(d_here, d_on, d_across)
    begin(u_here, u_keep)
    pass_rest(d_here, d_across)
    pass_last(d_on, d_across)
    settle(d_here, d_across, d_keep)

    @pl.loop(0, groups)
    def _(g):
        send_inner(g, 0, p_peer)

    pass_on(u_here, u_on, u_across)
    pass_rest(u_here, u_across)
    for cp in w_keep + w_out[:4]:
        cp.wait()

    @pl.loop(0, parts)
    def _(h):
        arrive(h, 0)
        far(h, 0)

    @pl.loop(0, groups)
    def _(g):
        forward(g, 0, q_peer)

    pass_last(u_on, u_across)
    for j in range(3):
        w_out[4 + j].wait()
        w_out[8 + j].wait()

    @pl.loop(0, parts)
    def _(h):
        early[part(h)] = jnp.dot(
            acts[0, part(h), 0:3 * width], w2[0:3 * width, 2 * width:],
            preferred_element_type=F32,
        )

    w_out[7].wait()
    w_out[11].wait()

    per = parts // groups

    @pl.loop(0, STEPS)
    def _(t):
        par = t % 2

        @pl.when(t > 0)
        def _():
            pl.semaphore_signal(pair, inc=1, device_id=mate, device_id_type=MESH)
            pl.semaphore_wait(pair, 1)

        @pl.loop(0, groups)
        def _(g):
            multiply(g * per, par, t == 0)

            @pl.when(t > 0)
            def _():
                forward(g, par)

            for i in range(1, per):
                multiply(g * per + i, par, t == 0)

        @pl.when(t == 0)
        def _():
            settle(u_here, u_across, u_keep)
            drain(d_here, d_on, d_across)
            drain(u_here, u_on, u_across)

        @pl.when(t > 0)
        def _():
            pl.semaphore_signal(pair, inc=1, device_id=mate, device_id_type=MESH)
            pl.semaphore_wait(pair, 1)

        @pl.loop(0, groups)
        def _(g):
            adapt(g, par)

            @pl.loop(0, per)
            def _(i):
                h = g * per + i
                finish(h, par)

                @pl.when(t < STEPS - 1)
                def _():
                    send_scaled(h, 1 - par)

                @pl.when(t == STEPS - 1)
                def _():
                    result(h).start()

            @pl.when(t < STEPS - 1)
            def _():
                send_inner(g, 1 - par)

    for h in range(parts):
        result(h).wait()


PARTS = 4
GROUPS = 2


def local(tokens, gain, base_weight, down, up, plan, target, slot):
    rows_all, width = tokens.shape
    owned, rank, _ = down.shape
    stores = 8
    lines = rows_all // GROUPS // 2 + 16
    dma = pltpu.SemaphoreType.DMA
    anywhere = pl.BlockSpec(memory_space=pl.ANY)
    return pl.pallas_call(
        functools.partial(kernel, PARTS, GROUPS),
        out_shape=jax.ShapeDtypeStruct((rows_all, width), BF),
        in_specs=[
            anywhere, anywhere, anywhere, anywhere, anywhere,
            anywhere, anywhere, anywhere,
        ],
        out_specs=anywhere,
        scratch_shapes=[
            pltpu.VMEM((4 * width, 4 * width), BF),
            pltpu.VMEM((stores, owned * rank, width), BF),
            pltpu.VMEM((stores, owned * rank, width), BF),
            pltpu.VMEM((2, rows_all, 4 * width), BF),
            pltpu.VMEM((2, GROUPS, 4, lines, 128), BF),
            pltpu.VMEM((2, 3, rows_all, width), BF),
            pltpu.VMEM((2, 3, rows_all, width), BF),
            pltpu.VMEM((2, GROUPS, lines, 128), BF),
            pltpu.VMEM((2, GROUPS, 3, lines, 128), BF),
            pltpu.VMEM((rows_all, width), F32),
            pltpu.VMEM((rows_all, 2 * width), F32),
            pltpu.VMEM((GROUPS, lines - 16, 128), F32),
            pltpu.VMEM((GROUPS, 8, 128), F32),
            pltpu.VMEM((rows_all, width), BF),
            pltpu.VMEM((rows_all, 128), F32),
            pltpu.VMEM((rows_all, width), BF),
            pltpu.VMEM((rows_all, 128), F32),
            pltpu.VMEM((1, width), F32),
            pltpu.VMEM((1, rows_all), jnp.int32),
            pltpu.VMEM((1, rows_all), jnp.int32),
            pltpu.SMEM((4, 8), jnp.int32),
            dma((5,)), dma((PARTS,)),
            dma((3, 4)), dma((3, 4)), dma((4,)),
            dma((2, 13)), dma((2, 13)), dma((2,)),
            dma((2, PARTS, 3)), dma((2, PARTS, 3)),
            dma((2, GROUPS, 3)), dma((2, GROUPS, 3)),
            dma((2, PARTS, 3)), dma((2, PARTS, 3)),
            dma((2, GROUPS, 3)), dma((2, GROUPS, 3)),
            pltpu.SemaphoreType.REGULAR,
        ],
        compiler_params=pltpu.CompilerParams(
            collective_id=0, has_side_effects=True, vmem_limit_bytes=56 << 20
        ),
    )(
        tokens, gain.reshape(1, -1), base_weight,
        down.reshape(owned * rank, width), up.reshape(owned * rank, width),
        plan.T, target.reshape(1, -1), slot.reshape(1, -1),
    )


def solution(mesh):
    return jax.shard_map(
        local,
        mesh=mesh,
        in_specs=(
            P("store", "mp"),
            P(),
            P(None, "mp"),
            P("store", None, "mp"),
            P("store", None, "mp"),
            P(),
            P("store", None),
            P("store"),
        ),
        out_specs=P("store", "mp"),
        check_vma=False,
    )
```

```python
import functools

import jax
import jax.numpy as jnp
from jax import lax
from jax.experimental import pallas as pl
from jax.experimental.pallas import tpu as pltpu
from jax.sharding import PartitionSpec as P

MESH = pl.DeviceIdType.MESH
STEPS = 4
SCALE = 0.5
EPS = 1e-05
HOPS = (2, 1, 3)
PLACE = {2: 0, 0: 1, 1: 2, 3: 3}
BF = jnp.bfloat16
F32 = jnp.float32


def kernel(
    parts, groups, tok, gain, w, down, up, plan, tgt, slt, out,
    w2, dn, un, acts, ext, sbuf, rbuf, xbuf, xrec, own, early, xown, sown, delta, scale, state, ids,
    gbuf, tbuf, sbuf_slot, pbuf, i_sem, o_sem,
    w_send, w_recv, w_loc, a_send, a_recv, a_loc,
    g_send, g_recv, e_send, e_recv, r_send, r_recv, x_send, x_recv, pair,
):
    rows_all, width = tok.shape
    rows = rows_all // parts
    block = rows_all // groups
    deep = block // 2
    slots = down.shape[0]
    half = slots // 2
    features = gain.shape[1]
    s = lax.axis_index("store")
    m = lax.axis_index("mp")
    z, c = s // 2, s % 2
    y, x = m // 4, m % 4
    p = x * (1 - c) + y * c
    q = y * (1 - c) + x * c

    def mp_of(pp, qq):
        return (qq * 4 + pp) * (1 - c) + (pp * 4 + qq) * c

    def p_peer(k):
        return (s, mp_of((p + k) % 4, q))

    def q_peer(k):
        return (s, mp_of(p, (q + k) % 4))

    def z_peer(k):
        return (((z + k) % 4) * 2 + c, m)

    mate = (z * 2 + 1 - c, m)

    def remote(src, dst, send, recv, device):
        return pltpu.make_async_remote_copy(
            src_ref=src, dst_ref=dst, send_sem=send, recv_sem=recv,
            device_id=device, device_id_type=MESH,
        )

    inputs = [
        pltpu.make_async_copy(tok, state, i_sem.at[0]),
        pltpu.make_async_copy(
            gain.at[:, pl.ds(pl.multiple_of(m * width, 128), width)], gbuf, i_sem.at[1]
        ),
        pltpu.make_async_copy(tgt, tbuf, i_sem.at[2]),
        pltpu.make_async_copy(slt, sbuf_slot, i_sem.at[3]),
        pltpu.make_async_copy(plan, pbuf, i_sem.at[4]),
    ]
    for cp in inputs:
        cp.start()

    barrier = pltpu.get_barrier_semaphore()
    for k in HOPS:
        pl.semaphore_signal(barrier, inc=1, device_id=p_peer(k), device_id_type=MESH)
        pl.semaphore_signal(barrier, inc=1, device_id=q_peer(k), device_id_type=MESH)
    for k in (1, 3):
        pl.semaphore_signal(barrier, inc=1, device_id=z_peer(k), device_id_type=MESH)
    pl.semaphore_signal(barrier, inc=1, device_id=mate, device_id_type=MESH)
    pl.semaphore_wait(barrier, 9)

    lo, hi = pl.ds(0, half), pl.ds(half, half)
    s_left, s_right, s_far = ((z + 3) % 4) * 2 + c, ((z + 1) % 4) * 2 + c, ((z + 2) % 4) * 2 + c

    def adapter_copies(f, src, dst):
        def go(i, a, b, device):
            return remote(a, b, a_send.at[f, i], a_recv.at[f, i], device)

        here = [
            go(0, src.at[lo], dst.at[s, lo], z_peer(1)),
            go(1, src.at[hi], dst.at[s, hi], z_peer(1)),
            go(2, src.at[hi], dst.at[s, hi], z_peer(3)),
            go(3, src.at[lo], dst.at[s, lo], z_peer(3)),
            go(4, src, dst.at[s], mate),
        ]
        on = [
            go(5, dst.at[s_left, lo], dst.at[s_left, lo], z_peer(1)),
            go(6, dst.at[s_right, hi], dst.at[s_right, hi], z_peer(3)),
        ]
        across = [
            go(7 + i, dst.at[o, part], dst.at[o, part], mate)
            for i, (o, part) in enumerate(
                ((s_left, lo), (s_right, hi), (s_left, hi), (s_right, lo), (s_far, lo), (s_far, hi))
            )
        ]
        keep = pltpu.make_async_copy(src, dst.at[s], a_loc.at[f])
        return here, on, across, keep

    d_here, d_on, d_across, d_keep = adapter_copies(0, down, dn)
    u_here, u_on, u_across, u_keep = adapter_copies(1, up, un)

    def begin(here, keep):
        for i in (0, 2, 1, 3, 4):
            here[i].start()
        keep.start()

    begin(d_here, d_keep)

    w_out = []
    for i, k in enumerate(HOPS):
        for j in range(4):
            first = pl.multiple_of(mp_of((p + j) % 4, (q + k) % 4) * width, 128)
            w_out.append(
                remote(
                    w.at[pl.ds(first, width)],
                    w2.at[pl.ds(j * width, width), pl.ds(PLACE[4 - k] * width, width)],
                    w_send.at[i, j], w_recv.at[i, j], q_peer(k),
                )
            )
    w_keep = []
    for j in range(4):
        first = pl.multiple_of(mp_of((p + j) % 4, q) * width, 128)
        w_keep.append(
            pltpu.make_async_copy(
                w.at[pl.ds(first, width)],
                w2.at[pl.ds(j * width, width), pl.ds(PLACE[0] * width, width)],
                w_loc.at[j],
            )
        )

    low = lax.broadcasted_iota(jnp.int32, (deep, 128), 1) < 64
    diagonal = lax.broadcasted_iota(jnp.int32, (block, 128), 0) == lax.broadcasted_iota(
        jnp.int32, (block, 128), 1
    )
    line = lax.broadcasted_iota(jnp.int32, (16, 128), 0)

    def part(h):
        return pl.ds(pl.multiple_of(h * rows, rows), rows)

    def group(g):
        return pl.ds(pl.multiple_of(g * block, block), block)

    def act_copies(h, par):
        return [
            remote(
                acts.at[par, part(h), pl.ds(0, width)],
                acts.at[par, part(h), pl.ds((4 - k) * width, width)],
                g_send.at[par, h, i], g_recv.at[par, h, i], p_peer(k),
            )
            for i, k in enumerate(HOPS)
        ]

    def ext_copies(g, par, peer=q_peer):
        return [
            remote(
                ext.at[par, g, 0], ext.at[par, g, 4 - k],
                e_send.at[par, g, i], e_recv.at[par, g, i], peer(k),
            )
            for i, k in enumerate(HOPS)
        ]

    def sum_copies(h, par):
        return [
            remote(
                sbuf.at[par, i, part(h)], rbuf.at[par, i, part(h)],
                r_send.at[par, h, i], r_recv.at[par, h, i], q_peer(k),
            )
            for i, k in enumerate(HOPS)
        ]

    def inner_copies(g, par, peer=p_peer):
        return [
            remote(
                xbuf.at[par, g], xrec.at[par, g, i],
                x_send.at[par, g, i], x_recv.at[par, g, i], peer(k),
            )
            for i, k in enumerate(HOPS)
        ]


    def send_scaled(h, par):
        acts[par, part(h), 0:width] = (state[part(h)].astype(F32) * gbuf[...]).astype(BF)
        for cp in act_copies(h, par):
            cp.start()

    def as_column(row):
        return jnp.sum(jnp.where(diagonal, row, 0.0), axis=1, keepdims=True)

    def packed(inner, square):
        top = square.astype(BF).astype(F32)
        tail = jnp.where(line == 0, top, jnp.where(line == 1, square - top, 0.0))
        return inner.astype(BF), tail.astype(BF)

    def send_inner(g, par, peer=q_peer):
        now = state[group(g)].astype(F32)
        square = jnp.sum(now * now, axis=1, keepdims=True)
        square = jnp.sum(jnp.where(diagonal, square, 0.0), axis=0, keepdims=True)
        mine = acts[par, group(g), 0:width]
        who = ids[group(g)]
        acc = jnp.zeros((block, 128), F32)
        for a in range(8):
            value = lax.dot_general(
                mine, dn[a], (((1,), (1,)), ((), ())), preferred_element_type=F32
            )
            for t in range(4):
                acc += jnp.where(
                    who == float(a * 8 + 2 * t), value[:, t * 128:(t + 1) * 128], 0.0
                )
        acc += pltpu.roll(acc, 64, 1)
        body, tail = packed(jnp.where(low, acc[:deep], acc[deep:]), square)
        ext[par, g, 0, 0:deep] = body
        ext[par, g, 0, deep:deep + 16] = tail
        for cp in ext_copies(g, par, peer):
            cp.start()

    def arrive(h, par):
        for cp in act_copies(h, par):
            cp.wait()

    def far(h, par):
        value = jnp.dot(acts[par, part(h)], w2[:, 0:2 * width], preferred_element_type=F32)
        sbuf[par, 0, part(h)] = value[:, :width].astype(BF)
        sum_copies(h, par)[0].start()
        own[part(h)] = value[:, width:]

    def send_near(h, par, value):
        copies = sum_copies(h, par)
        value = value.astype(BF)
        sbuf[par, 1, part(h)] = value[:, :width]
        copies[1].start()
        sbuf[par, 2, part(h)] = value[:, width:]
        copies[2].start()

    def multiply(h, par, first):
        @pl.when(jnp.logical_not(first))
        def _():
            arrive(h, par)
            far(h, par)
            send_near(
                h, par,
                jnp.dot(acts[par, part(h)], w2[:, 2 * width:], preferred_element_type=F32),
            )

        @pl.when(first)
        def _():
            last = jnp.dot(
                acts[par, part(h), 3 * width:], w2[3 * width:, 2 * width:],
                preferred_element_type=F32,
            )
            send_near(h, par, early[part(h)] + last)

    def forward(g, par, peer=p_peer):
        for cp in ext_copies(g, par):
            cp.wait()
        both = ext[par, g, 0].astype(F32)
        for i in range(1, 4):
            both += ext[par, g, i].astype(F32)
        inner, square = both[:deep], both[deep:deep + 1] + both[deep + 1:deep + 2]
        body, tail = packed(inner, square)
        xbuf[par, g, 0:deep] = body
        xbuf[par, g, deep:deep + 16] = tail
        for cp in inner_copies(g, par, peer):
            cp.start()
        xown[g] = inner
        sown[g] = jnp.broadcast_to(square, (8, 128))

    def adapt(g, par):
        for cp in inner_copies(g, par):
            cp.wait()
        both = xrec[par, g, 0].astype(F32)
        for i in range(1, 3):
            both += xrec[par, g, i].astype(F32)
        square = both[deep:deep + 1] + both[deep + 1:deep + 2] + sown[g, 0:1]
        factor = as_column(lax.rsqrt(square * (1.0 / features) + EPS))
        scale[group(g)] = jnp.broadcast_to(factor, (block, 128))
        inner = both[:deep] + xown[g]
        other = pltpu.roll(inner, 64, 1)
        inner = jnp.concatenate([jnp.where(low, inner, other), jnp.where(low, other, inner)], 0)
        inner = (inner * factor).astype(BF).astype(F32)
        who = ids[group(g)]
        outer = jnp.zeros((block, width), F32)
        for a in range(8):
            spread = jnp.concatenate(
                [
                    jnp.where(who == float(a * 8 + 2 * t), inner, 0.0).astype(BF)
                    for t in range(4)
                ],
                axis=1,
            )
            outer += jnp.dot(spread, un[a], preferred_element_type=F32)
        delta[group(g)] = (SCALE * outer).astype(BF)

    def finish(h, par):
        for cp in sum_copies(h, par):
            cp.wait()
        base = own[part(h)]
        for i in range(3):
            base += rbuf[par, i, part(h)].astype(F32)
        factor = jnp.concatenate([scale[part(h)]] * (width // 128), axis=1)
        now = state[part(h)].astype(F32) + base * factor + delta[part(h)].astype(F32)
        state[part(h)] = now.astype(BF)

    def result(h):
        return pltpu.make_async_copy(state.at[part(h)], out.at[part(h)], o_sem.at[h])

    for j in range(4):
        w_out[j].start()
    for cp in w_keep:
        cp.start()

    inputs[0].wait()
    inputs[1].wait()

    @pl.loop(0, parts)
    def _(h):
        send_scaled(h, 0)

    for j in range(4):
        for i in (1, 2):
            w_out[i * 4 + j].start()

    inputs[2].wait()
    inputs[3].wait()
    inputs[4].wait()
    wanted = tbuf[...]
    place = sbuf_slot[...]
    key = wanted * 4 + place - 8
    chosen = wanted * 8 + place
    for a in range(8):
        for r in range(4):
            hit = jnp.logical_and(place >= 8, key == a * 4 + r)
            chosen = jnp.where(hit, pbuf[r, a], chosen)
    chosen = chosen.astype(F32)
    upper = (lax.broadcasted_iota(jnp.int32, (block, 128), 1) >= 64).astype(F32)
    for g in range(groups):
        ids[g * block:(g + 1) * block] = as_column(chosen[:, g * block:(g + 1) * block]) - upper

    def pass_on(here, on, across):
        here[0].wait_recv()
        on[0].start()
        across[0].start()
        here[2].wait_recv()
        on[1].start()
        across[1].start()

    def pass_rest(here, across):
        here[1].wait_recv()
        across[2].start()
        here[3].wait_recv()
        across[3].start()

    def pass_last(on, across):
        on[0].wait_recv()
        across[4].start()
        on[1].wait_recv()
        across[5].start()

    def settle(here, across, keep):
        here[4].wait_recv()
        keep.wait()
        for cp in across:
            cp.wait_recv()

    def drain(here, on, across):
        for cp in here + on + across:
            cp.wait_send()

    pass_on(d_here, d_on, d_across)
    begin(u_here, u_keep)
    pass_rest(d_here, d_across)
    pass_last(d_on, d_across)
    settle(d_here, d_across, d_keep)

    @pl.loop(0, groups)
    def _(g):
        send_inner(g, 0, p_peer)

    pass_on(u_here, u_on, u_across)
    for cp in w_keep + w_out[:4]:
        cp.wait()

    @pl.loop(0, parts)
    def _(h):
        arrive(h, 0)
        far(h, 0)

    @pl.loop(0, groups)
    def _(g):
        forward(g, 0, q_peer)

    pass_rest(u_here, u_across)
    pass_last(u_on, u_across)
    for j in range(3):
        w_out[4 + j].wait()
        w_out[8 + j].wait()

    @pl.loop(0, parts)
    def _(h):
        early[part(h)] = jnp.dot(
            acts[0, part(h), 0:3 * width], w2[0:3 * width, 2 * width:],
            preferred_element_type=F32,
        )

    w_out[7].wait()
    w_out[11].wait()

    per = parts // groups

    @pl.loop(0, STEPS)
    def _(t):
        par = t % 2

        @pl.when(t > 0)
        def _():
            pl.semaphore_signal(pair, inc=1, device_id=mate, device_id_type=MESH)
            pl.semaphore_wait(pair, 1)

        @pl.loop(0, groups)
        def _(g):
            multiply(g * per, par, t == 0)

            @pl.when(t > 0)
            def _():
                forward(g, par)

            for i in range(1, per):
                multiply(g * per + i, par, t == 0)

        @pl.when(t == 0)
        def _():
            settle(u_here, u_across, u_keep)
            drain(d_here, d_on, d_across)
            drain(u_here, u_on, u_across)

        @pl.when(t > 0)
        def _():
            pl.semaphore_signal(pair, inc=1, device_id=mate, device_id_type=MESH)
            pl.semaphore_wait(pair, 1)

        @pl.loop(0, groups)
        def _(g):
            adapt(g, par)

            @pl.loop(0, per)
            def _(i):
                h = g * per + i
                finish(h, par)

                @pl.when(t < STEPS - 1)
                def _():
                    send_scaled(h, 1 - par)

                @pl.when(t == STEPS - 1)
                def _():
                    result(h).start()

            @pl.when(t < STEPS - 1)
            def _():
                send_inner(g, 1 - par)

    for h in range(parts):
        result(h).wait()


PARTS = 4
GROUPS = 2


def local(tokens, gain, base_weight, down, up, plan, target, slot):
    rows_all, width = tokens.shape
    owned, rank, _ = down.shape
    stores = 8
    lines = rows_all // GROUPS // 2 + 16
    dma = pltpu.SemaphoreType.DMA
    anywhere = pl.BlockSpec(memory_space=pl.ANY)
    return pl.pallas_call(
        functools.partial(kernel, PARTS, GROUPS),
        out_shape=jax.ShapeDtypeStruct((rows_all, width), BF),
        in_specs=[
            anywhere, anywhere, anywhere, anywhere, anywhere,
            anywhere, anywhere, anywhere,
        ],
        out_specs=anywhere,
        scratch_shapes=[
            pltpu.VMEM((4 * width, 4 * width), BF),
            pltpu.VMEM((stores, owned * rank, width), BF),
            pltpu.VMEM((stores, owned * rank, width), BF),
            pltpu.VMEM((2, rows_all, 4 * width), BF),
            pltpu.VMEM((2, GROUPS, 4, lines, 128), BF),
            pltpu.VMEM((2, 3, rows_all, width), BF),
            pltpu.VMEM((2, 3, rows_all, width), BF),
            pltpu.VMEM((2, GROUPS, lines, 128), BF),
            pltpu.VMEM((2, GROUPS, 3, lines, 128), BF),
            pltpu.VMEM((rows_all, width), F32),
            pltpu.VMEM((rows_all, 2 * width), F32),
            pltpu.VMEM((GROUPS, lines - 16, 128), F32),
            pltpu.VMEM((GROUPS, 8, 128), F32),
            pltpu.VMEM((rows_all, width), BF),
            pltpu.VMEM((rows_all, 128), F32),
            pltpu.VMEM((rows_all, width), BF),
            pltpu.VMEM((rows_all, 128), F32),
            pltpu.VMEM((1, width), F32),
            pltpu.VMEM((1, rows_all), jnp.int32),
            pltpu.VMEM((1, rows_all), jnp.int32),
            pltpu.SMEM((4, 8), jnp.int32),
            dma((5,)), dma((PARTS,)),
            dma((3, 4)), dma((3, 4)), dma((4,)),
            dma((2, 13)), dma((2, 13)), dma((2,)),
            dma((2, PARTS, 3)), dma((2, PARTS, 3)),
            dma((2, GROUPS, 3)), dma((2, GROUPS, 3)),
            dma((2, PARTS, 3)), dma((2, PARTS, 3)),
            dma((2, GROUPS, 3)), dma((2, GROUPS, 3)),
            pltpu.SemaphoreType.REGULAR,
        ],
        compiler_params=pltpu.CompilerParams(
            collective_id=0, has_side_effects=True, vmem_limit_bytes=56 << 20
        ),
    )(
        tokens, gain.reshape(1, -1), base_weight,
        down.reshape(owned * rank, width), up.reshape(owned * rank, width),
        plan.T, target.reshape(1, -1), slot.reshape(1, -1),
    )


def solution(mesh):
    return jax.shard_map(
        local,
        mesh=mesh,
        in_specs=(
            P("store", "mp"),
            P(),
            P(None, "mp"),
            P("store", None, "mp"),
            P("store", None, "mp"),
            P(),
            P("store", None),
            P("store"),
        ),
        out_specs=P("store", "mp"),
        check_vma=False,
    )
```

```python
import functools

import jax
import jax.numpy as jnp
from jax import lax
from jax.experimental import pallas as pl
from jax.experimental.pallas import tpu as pltpu
from jax.sharding import PartitionSpec as P

MESH = pl.DeviceIdType.MESH
STEPS = 4
SCALE = 0.5
EPS = 1e-05
HOPS = (2, 1, 3)
PLACE = {2: 0, 0: 1, 1: 2, 3: 3}
BF = jnp.bfloat16
F32 = jnp.float32


def kernel(
    parts, groups, tok, gain, w, down, up, plan, tgt, slt, out,
    w2, dn, un, acts, ext, sbuf, rbuf, xbuf, xrec, own, early, xown, sown, delta, scale, state, ids,
    gbuf, tbuf, sbuf_slot, pbuf, i_sem, o_sem,
    w_send, w_recv, w_loc, a_send, a_recv, a_loc,
    g_send, g_recv, e_send, e_recv, r_send, r_recv, x_send, x_recv, pair,
):
    rows_all, width = tok.shape
    rows = rows_all // parts
    block = rows_all // groups
    deep = block // 2
    slots = down.shape[0]
    half = slots // 2
    features = gain.shape[1]
    s = lax.axis_index("store")
    m = lax.axis_index("mp")
    z, c = s // 2, s % 2
    y, x = m // 4, m % 4
    p = x * (1 - c) + y * c
    q = y * (1 - c) + x * c

    def mp_of(pp, qq):
        return (qq * 4 + pp) * (1 - c) + (pp * 4 + qq) * c

    def p_peer(k):
        return (s, mp_of((p + k) % 4, q))

    def q_peer(k):
        return (s, mp_of(p, (q + k) % 4))

    def z_peer(k):
        return (((z + k) % 4) * 2 + c, m)

    mate = (z * 2 + 1 - c, m)

    def remote(src, dst, send, recv, device):
        return pltpu.make_async_remote_copy(
            src_ref=src, dst_ref=dst, send_sem=send, recv_sem=recv,
            device_id=device, device_id_type=MESH,
        )

    inputs = [
        pltpu.make_async_copy(tok, state, i_sem.at[0]),
        pltpu.make_async_copy(
            gain.at[:, pl.ds(pl.multiple_of(m * width, 128), width)], gbuf, i_sem.at[1]
        ),
        pltpu.make_async_copy(tgt, tbuf, i_sem.at[2]),
        pltpu.make_async_copy(slt, sbuf_slot, i_sem.at[3]),
        pltpu.make_async_copy(plan, pbuf, i_sem.at[4]),
    ]
    for cp in inputs:
        cp.start()

    barrier = pltpu.get_barrier_semaphore()
    for k in HOPS:
        pl.semaphore_signal(barrier, inc=1, device_id=p_peer(k), device_id_type=MESH)
        pl.semaphore_signal(barrier, inc=1, device_id=q_peer(k), device_id_type=MESH)
    for k in (1, 3):
        pl.semaphore_signal(barrier, inc=1, device_id=z_peer(k), device_id_type=MESH)
    pl.semaphore_signal(barrier, inc=1, device_id=mate, device_id_type=MESH)
    pl.semaphore_wait(barrier, 9)

    lo, hi = pl.ds(0, half), pl.ds(half, half)
    s_left, s_right, s_far = ((z + 3) % 4) * 2 + c, ((z + 1) % 4) * 2 + c, ((z + 2) % 4) * 2 + c

    def adapter_copies(f, src, dst):
        def go(i, a, b, device):
            return remote(a, b, a_send.at[f, i], a_recv.at[f, i], device)

        here = [
            go(0, src.at[lo], dst.at[s, lo], z_peer(1)),
            go(1, src.at[hi], dst.at[s, hi], z_peer(1)),
            go(2, src.at[hi], dst.at[s, hi], z_peer(3)),
            go(3, src.at[lo], dst.at[s, lo], z_peer(3)),
            go(4, src, dst.at[s], mate),
        ]
        on = [
            go(5, dst.at[s_left, lo], dst.at[s_left, lo], z_peer(1)),
            go(6, dst.at[s_right, hi], dst.at[s_right, hi], z_peer(3)),
        ]
        across = [
            go(7 + i, dst.at[o, part], dst.at[o, part], mate)
            for i, (o, part) in enumerate(
                ((s_left, lo), (s_right, hi), (s_left, hi), (s_right, lo), (s_far, lo), (s_far, hi))
            )
        ]
        keep = pltpu.make_async_copy(src, dst.at[s], a_loc.at[f])
        return here, on, across, keep

    d_here, d_on, d_across, d_keep = adapter_copies(0, down, dn)
    u_here, u_on, u_across, u_keep = adapter_copies(1, up, un)

    def begin(here, keep):
        for i in (0, 2, 1, 3, 4):
            here[i].start()
        keep.start()

    begin(d_here, d_keep)

    w_out = []
    for i, k in enumerate(HOPS):
        for j in range(4):
            first = pl.multiple_of(mp_of((p + j) % 4, (q + k) % 4) * width, 128)
            w_out.append(
                remote(
                    w.at[pl.ds(first, width)],
                    w2.at[pl.ds(j * width, width), pl.ds(PLACE[4 - k] * width, width)],
                    w_send.at[i, j], w_recv.at[i, j], q_peer(k),
                )
            )
    w_keep = []
    for j in range(4):
        first = pl.multiple_of(mp_of((p + j) % 4, q) * width, 128)
        w_keep.append(
            pltpu.make_async_copy(
                w.at[pl.ds(first, width)],
                w2.at[pl.ds(j * width, width), pl.ds(PLACE[0] * width, width)],
                w_loc.at[j],
            )
        )

    low = lax.broadcasted_iota(jnp.int32, (deep, 128), 1) < 64
    diagonal = lax.broadcasted_iota(jnp.int32, (block, 128), 0) == lax.broadcasted_iota(
        jnp.int32, (block, 128), 1
    )
    line = lax.broadcasted_iota(jnp.int32, (16, 128), 0)

    def part(h):
        return pl.ds(pl.multiple_of(h * rows, rows), rows)

    def group(g):
        return pl.ds(pl.multiple_of(g * block, block), block)

    def act_copies(h, par):
        return [
            remote(
                acts.at[par, part(h), pl.ds(0, width)],
                acts.at[par, part(h), pl.ds((4 - k) * width, width)],
                g_send.at[par, h, i], g_recv.at[par, h, i], p_peer(k),
            )
            for i, k in enumerate(HOPS)
        ]

    def ext_copies(g, par, peer=q_peer):
        return [
            remote(
                ext.at[par, g, 0], ext.at[par, g, 4 - k],
                e_send.at[par, g, i], e_recv.at[par, g, i], peer(k),
            )
            for i, k in enumerate(HOPS)
        ]

    def sum_copies(h, par):
        return [
            remote(
                sbuf.at[par, i, part(h)], rbuf.at[par, i, part(h)],
                r_send.at[par, h, i], r_recv.at[par, h, i], q_peer(k),
            )
            for i, k in enumerate(HOPS)
        ]

    def inner_copies(g, par, peer=p_peer):
        return [
            remote(
                xbuf.at[par, g], xrec.at[par, g, i],
                x_send.at[par, g, i], x_recv.at[par, g, i], peer(k),
            )
            for i, k in enumerate(HOPS)
        ]


    def send_scaled(h, par):
        acts[par, part(h), 0:width] = (state[part(h)].astype(F32) * gbuf[...]).astype(BF)
        for cp in act_copies(h, par):
            cp.start()

    def as_column(row):
        return jnp.sum(jnp.where(diagonal, row, 0.0), axis=1, keepdims=True)

    def packed(inner, square):
        top = square.astype(BF).astype(F32)
        tail = jnp.where(line == 0, top, jnp.where(line == 1, square - top, 0.0))
        return inner.astype(BF), tail.astype(BF)

    def send_inner(g, par, peer=q_peer):
        now = state[group(g)].astype(F32)
        square = jnp.sum(now * now, axis=1, keepdims=True)
        square = jnp.sum(jnp.where(diagonal, square, 0.0), axis=0, keepdims=True)
        mine = acts[par, group(g), 0:width]
        who = ids[group(g)]
        acc = jnp.zeros((block, 128), F32)
        for a in range(8):
            value = lax.dot_general(
                mine, dn[a], (((1,), (1,)), ((), ())), preferred_element_type=F32
            )
            for t in range(4):
                acc += jnp.where(
                    who == float(a * 8 + 2 * t), value[:, t * 128:(t + 1) * 128], 0.0
                )
        acc += pltpu.roll(acc, 64, 1)
        body, tail = packed(jnp.where(low, acc[:deep], acc[deep:]), square)
        ext[par, g, 0, 0:deep] = body
        ext[par, g, 0, deep:deep + 16] = tail
        for cp in ext_copies(g, par, peer):
            cp.start()

    def arrive(h, par):
        for cp in act_copies(h, par):
            cp.wait()

    def far(h, par):
        value = jnp.dot(acts[par, part(h)], w2[:, 0:2 * width], preferred_element_type=F32)
        sbuf[par, 0, part(h)] = value[:, :width].astype(BF)
        sum_copies(h, par)[0].start()
        own[part(h)] = value[:, width:]

    def send_near(h, par, value):
        copies = sum_copies(h, par)
        value = value.astype(BF)
        sbuf[par, 1, part(h)] = value[:, :width]
        copies[1].start()
        sbuf[par, 2, part(h)] = value[:, width:]
        copies[2].start()

    def multiply(h, par, first):
        @pl.when(jnp.logical_not(first))
        def _():
            arrive(h, par)

            @pl.when(h == 0)
            def _():
                pl.semaphore_signal(pair, inc=1, device_id=mate, device_id_type=MESH)
                pl.semaphore_wait(pair, 1)

            far(h, par)
            send_near(
                h, par,
                jnp.dot(acts[par, part(h)], w2[:, 2 * width:], preferred_element_type=F32),
            )

        @pl.when(first)
        def _():
            last = jnp.dot(
                acts[par, part(h), 3 * width:], w2[3 * width:, 2 * width:],
                preferred_element_type=F32,
            )
            send_near(h, par, early[part(h)] + last)

    def forward(g, par, peer=p_peer):
        for cp in ext_copies(g, par):
            cp.wait()
        both = ext[par, g, 0].astype(F32)
        for i in range(1, 4):
            both += ext[par, g, i].astype(F32)
        inner, square = both[:deep], both[deep:deep + 1] + both[deep + 1:deep + 2]
        body, tail = packed(inner, square)
        xbuf[par, g, 0:deep] = body
        xbuf[par, g, deep:deep + 16] = tail
        for cp in inner_copies(g, par, peer):
            cp.start()
        xown[g] = inner
        sown[g] = jnp.broadcast_to(square, (8, 128))

    def adapt(g, par):
        for cp in inner_copies(g, par):
            cp.wait()
        both = xrec[par, g, 0].astype(F32)
        for i in range(1, 3):
            both += xrec[par, g, i].astype(F32)
        square = both[deep:deep + 1] + both[deep + 1:deep + 2] + sown[g, 0:1]
        factor = as_column(lax.rsqrt(square * (1.0 / features) + EPS))
        scale[group(g)] = jnp.broadcast_to(factor, (block, 128))
        inner = both[:deep] + xown[g]
        other = pltpu.roll(inner, 64, 1)
        inner = jnp.concatenate([jnp.where(low, inner, other), jnp.where(low, other, inner)], 0)
        inner = (inner * factor).astype(BF).astype(F32)
        who = ids[group(g)]
        outer = jnp.zeros((block, width), F32)
        for a in range(8):
            spread = jnp.concatenate(
                [
                    jnp.where(who == float(a * 8 + 2 * t), inner, 0.0).astype(BF)
                    for t in range(4)
                ],
                axis=1,
            )
            outer += jnp.dot(spread, un[a], preferred_element_type=F32)
        delta[group(g)] = (SCALE * outer).astype(BF)

    def finish(h, par):
        for cp in sum_copies(h, par):
            cp.wait()
        base = own[part(h)]
        for i in range(3):
            base += rbuf[par, i, part(h)].astype(F32)
        factor = jnp.concatenate([scale[part(h)]] * (width // 128), axis=1)
        now = state[part(h)].astype(F32) + base * factor + delta[part(h)].astype(F32)
        state[part(h)] = now.astype(BF)

    def result(h):
        return pltpu.make_async_copy(state.at[part(h)], out.at[part(h)], o_sem.at[h])

    for j in range(4):
        w_out[j].start()
    for cp in w_keep:
        cp.start()

    inputs[0].wait()
    inputs[1].wait()

    @pl.loop(0, parts)
    def _(h):
        send_scaled(h, 0)

    for j in range(4):
        for i in (1, 2):
            w_out[i * 4 + j].start()

    inputs[2].wait()
    inputs[3].wait()
    inputs[4].wait()
    wanted = tbuf[...]
    place = sbuf_slot[...]
    key = wanted * 4 + place - 8
    chosen = wanted * 8 + place
    for a in range(8):
        for r in range(4):
            hit = jnp.logical_and(place >= 8, key == a * 4 + r)
            chosen = jnp.where(hit, pbuf[r, a], chosen)
    chosen = chosen.astype(F32)
    upper = (lax.broadcasted_iota(jnp.int32, (block, 128), 1) >= 64).astype(F32)
    for g in range(groups):
        ids[g * block:(g + 1) * block] = as_column(chosen[:, g * block:(g + 1) * block]) - upper

    def pass_on(here, on, across):
        here[0].wait_recv()
        on[0].start()
        across[0].start()
        here[2].wait_recv()
        on[1].start()
        across[1].start()

    def pass_rest(here, across):
        here[1].wait_recv()
        across[2].start()
        here[3].wait_recv()
        across[3].start()

    def pass_last(on, across):
        on[0].wait_recv()
        across[4].start()
        on[1].wait_recv()
        across[5].start()

    def settle(here, across, keep):
        here[4].wait_recv()
        keep.wait()
        for cp in across:
            cp.wait_recv()

    def drain(here, on, across):
        for cp in here + on + across:
            cp.wait_send()

    pass_on(d_here, d_on, d_across)
    begin(u_here, u_keep)
    pass_rest(d_here, d_across)
    pass_last(d_on, d_across)
    settle(d_here, d_across, d_keep)

    @pl.loop(0, groups)
    def _(g):
        send_inner(g, 0, p_peer)

    pass_on(u_here, u_on, u_across)
    for cp in w_keep + w_out[:4]:
        cp.wait()

    @pl.loop(0, parts)
    def _(h):
        arrive(h, 0)
        far(h, 0)

    @pl.loop(0, groups)
    def _(g):
        forward(g, 0, q_peer)

    pass_rest(u_here, u_across)
    pass_last(u_on, u_across)
    for j in range(3):
        w_out[4 + j].wait()
        w_out[8 + j].wait()

    @pl.loop(0, parts)
    def _(h):
        early[part(h)] = jnp.dot(
            acts[0, part(h), 0:3 * width], w2[0:3 * width, 2 * width:],
            preferred_element_type=F32,
        )

    w_out[7].wait()
    w_out[11].wait()

    per = parts // groups

    @pl.loop(0, STEPS)
    def _(t):
        par = t % 2

        @pl.loop(0, groups)
        def _(g):
            multiply(g * per, par, t == 0)

            @pl.when(t > 0)
            def _():
                forward(g, par)

            for i in range(1, per):
                multiply(g * per + i, par, t == 0)

        @pl.when(t == 0)
        def _():
            settle(u_here, u_across, u_keep)
            drain(d_here, d_on, d_across)
            drain(u_here, u_on, u_across)

        @pl.when(t > 0)
        def _():
            pl.semaphore_signal(pair, inc=1, device_id=mate, device_id_type=MESH)
            pl.semaphore_wait(pair, 1)

        @pl.loop(0, groups)
        def _(g):
            adapt(g, par)

            @pl.loop(0, per)
            def _(i):
                h = g * per + i
                finish(h, par)

                @pl.when(t < STEPS - 1)
                def _():
                    send_scaled(h, 1 - par)

                @pl.when(t == STEPS - 1)
                def _():
                    result(h).start()

            @pl.when(t < STEPS - 1)
            def _():
                send_inner(g, 1 - par)

    for h in range(parts):
        result(h).wait()


PARTS = 4
GROUPS = 2


def local(tokens, gain, base_weight, down, up, plan, target, slot):
    rows_all, width = tokens.shape
    owned, rank, _ = down.shape
    stores = 8
    lines = rows_all // GROUPS // 2 + 16
    dma = pltpu.SemaphoreType.DMA
    anywhere = pl.BlockSpec(memory_space=pl.ANY)
    return pl.pallas_call(
        functools.partial(kernel, PARTS, GROUPS),
        out_shape=jax.ShapeDtypeStruct((rows_all, width), BF),
        in_specs=[
            anywhere, anywhere, anywhere, anywhere, anywhere,
            anywhere, anywhere, anywhere,
        ],
        out_specs=anywhere,
        scratch_shapes=[
            pltpu.VMEM((4 * width, 4 * width), BF),
            pltpu.VMEM((stores, owned * rank, width), BF),
            pltpu.VMEM((stores, owned * rank, width), BF),
            pltpu.VMEM((2, rows_all, 4 * width), BF),
            pltpu.VMEM((2, GROUPS, 4, lines, 128), BF),
            pltpu.VMEM((2, 3, rows_all, width), BF),
            pltpu.VMEM((2, 3, rows_all, width), BF),
            pltpu.VMEM((2, GROUPS, lines, 128), BF),
            pltpu.VMEM((2, GROUPS, 3, lines, 128), BF),
            pltpu.VMEM((rows_all, width), F32),
            pltpu.VMEM((rows_all, 2 * width), F32),
            pltpu.VMEM((GROUPS, lines - 16, 128), F32),
            pltpu.VMEM((GROUPS, 8, 128), F32),
            pltpu.VMEM((rows_all, width), BF),
            pltpu.VMEM((rows_all, 128), F32),
            pltpu.VMEM((rows_all, width), BF),
            pltpu.VMEM((rows_all, 128), F32),
            pltpu.VMEM((1, width), F32),
            pltpu.VMEM((1, rows_all), jnp.int32),
            pltpu.VMEM((1, rows_all), jnp.int32),
            pltpu.SMEM((4, 8), jnp.int32),
            dma((5,)), dma((PARTS,)),
            dma((3, 4)), dma((3, 4)), dma((4,)),
            dma((2, 13)), dma((2, 13)), dma((2,)),
            dma((2, PARTS, 3)), dma((2, PARTS, 3)),
            dma((2, GROUPS, 3)), dma((2, GROUPS, 3)),
            dma((2, PARTS, 3)), dma((2, PARTS, 3)),
            dma((2, GROUPS, 3)), dma((2, GROUPS, 3)),
            pltpu.SemaphoreType.REGULAR,
        ],
        compiler_params=pltpu.CompilerParams(
            collective_id=0, has_side_effects=True, vmem_limit_bytes=56 << 20
        ),
    )(
        tokens, gain.reshape(1, -1), base_weight,
        down.reshape(owned * rank, width), up.reshape(owned * rank, width),
        plan.T, target.reshape(1, -1), slot.reshape(1, -1),
    )


def solution(mesh):
    return jax.shard_map(
        local,
        mesh=mesh,
        in_specs=(
            P("store", "mp"),
            P(),
            P(None, "mp"),
            P("store", None, "mp"),
            P("store", None, "mp"),
            P(),
            P("store", None),
            P("store"),
        ),
        out_specs=P("store", "mp"),
        check_vma=False,
    )
```
